256 devices in a mesh: dp: 64 (over z, y, core), tensor: 4 (over x).
Axes of the slice: x: 4, y: 4, z: 8, core: 2. Of those that a mesh axis runs over, the one named last changes fastest.
Arguments:
- inputs: bfloat16 [45056, 1280], P('dp'), may hold values from -24 to 24
- targets: bfloat16 [45056, 1280], P('dp'), may hold values from -6 to 6
- w_in: bfloat16 [1280, 5120], P(None, 'tensor'), may hold values from -0.15625 to 0.15625
- w_out: bfloat16 [5120, 1280], P('tensor'), may hold values from -0.078125 to 0.078125
Outputs:
- merged_in: float32 [1280, 5120], P('dp', 'tensor')
- merged_out: float32 [1280, 5120], P('dp', 'tensor')
The draws below stay inside these ranges and needn't reach their ends.
All inputs are finite; a program needn't handle non-finite values.
Results may differ from the reference program's by a relative error of at most 0.0033.
Values may be sent and summed in bfloat16 or wider, within the bound.
A program may use at most 128 MiB of HBM per device.

```python
import jax
import jax.numpy as jnp

D = 1280
FF = 5120
ROWS_DEV = 704
ROWS = 45056
N_DP = 64


def draw_inputs(key, part):
    first_key = jax.random.fold_in(jax.random.fold_in(key, 17), 0)
    base = jnp.clip(jax.random.normal(first_key, (ROWS, D), jnp.float32), -4.0, 4.0)
    blocks = ROWS // ROWS_DEV
    block_of = jnp.arange(ROWS) // ROWS_DEV
    row_scale = 1.0 + 2.0 * block_of.astype(jnp.float32) / max(blocks - 1, 1)
    return (base * row_scale[:, None]).astype(jnp.bfloat16)


def steps_of(own_key, dims, cuts, low, high):
    def one(axis_at, blocks):
        steps = jax.random.uniform(jax.random.fold_in(jax.random.fold_in(own_key, 6), axis_at), (blocks,), jnp.float32, low / len(cuts), high / len(cuts))
        return jnp.repeat(jnp.exp(steps), dims[axis_at] // blocks).reshape((-1,) + (1,) * (len(dims) - axis_at - 1))

    level = one(*cuts[0])
    for cut in cuts[1:]:
        level = level * one(*cut)
    return level


def scatter_about(key, extent, width, reach, shards=(), kind=jnp.bfloat16):
    entries = jax.random.normal(key, extent, jnp.float32) * width
    if len(shards) > 0:
        entries = steps_of(key, extent, shards, -0.22, 0.18) * entries
    return jnp.clip(entries, min=-reach, max=reach).astype(kind)


def setup_inputs(seed: int = 0) -> dict:
    key_of = jax.random.split(jax.random.key(seed), 5)
    return {
        "inputs": draw_inputs(jax.random.fold_in(key_of[4], 71), 0),
        "targets": scatter_about(key_of[1], (ROWS, D), 1.0, 6.0, ((0, 64),)),
        "w_in": scatter_about(key_of[2], (D, FF), D ** -0.5, 0.15625, ((1, 4),)),
        "w_out": scatter_about(key_of[3], (FF, D), FF ** -0.5, 0.078125, ((0, 4),)),
    }


def activate(values):
    return jax.nn.gelu(values, approximate=True)

def worker_grads(inputs, targets, w_in, w_out):
    preact = jnp.dot(inputs, w_in, preferred_element_type=jnp.float32)
    hidden = activate(preact).astype(jnp.bfloat16)
    output = jnp.dot(hidden, w_out, preferred_element_type=jnp.float32)
    error = ((output - targets.astype(jnp.float32)) / ROWS_DEV).astype(jnp.bfloat16)
    back = jnp.dot(error, w_out.T, preferred_element_type=jnp.float32)
    _, pullback = jax.vjp(activate, preact)
    dpre = pullback(back)[0].astype(jnp.bfloat16)
    first = jnp.dot(inputs.T, dpre, preferred_element_type=jnp.float32)
    second = jnp.dot(error.T, hidden, preferred_element_type=jnp.float32)
    return (first, second)

def merge_pair(lower, higher):
    product = jnp.sum(lower[0] * higher[0]) + jnp.sum(lower[1] * higher[1])
    norm_low = jnp.sum(lower[0] * lower[0]) + jnp.sum(lower[1] * lower[1])
    norm_high = jnp.sum(higher[0] * higher[0]) + jnp.sum(higher[1] * higher[1])
    coef_low = 1.0 - product / (2.0 * (norm_low + 1e-06))
    coef_high = 1.0 - product / (2.0 * (norm_high + 1e-06))
    return (coef_low * lower[0] + coef_high * higher[0], coef_low * lower[1] + coef_high * higher[1])

def subtree(residue, stride, inputs, targets, w_in, w_out):
    if stride == N_DP:
        start = residue * ROWS_DEV
        return worker_grads(inputs[start:start + ROWS_DEV], targets[start:start + ROWS_DEV], w_in, w_out)
    lower = subtree(residue, 2 * stride, inputs, targets, w_in, w_out)
    higher = subtree(residue + stride, 2 * stride, inputs, targets, w_in, w_out)
    return merge_pair(lower, higher)

def reference(inputs, targets, w_in, w_out):
    merged = subtree(0, 1, inputs, targets, w_in, w_out)
    return (merged[0], merged[1])
```

```python
import functools
import math

import jax
import jax.numpy as jnp
from jax import lax
from jax.experimental import pallas as pl
from jax.experimental.pallas import tpu as pltpu
from jax.sharding import PartitionSpec as P

F32, BF16 = jnp.float32, jnp.bfloat16
EPSILON = 1e-06
GELU_A = math.sqrt(2.0 / math.pi)
GELU_B = 0.044715
MESH = pl.DeviceIdType.MESH
BY_ROWS = (((1,), (1,)), ((), ()))


def tile_of(n):
    return 256 if n % 256 == 0 else n


def block(start, size, step):
    return pl.ds(pl.multiple_of(start, step), size)


def fold(v):
    rows, columns = v.shape
    t = v[0:8]
    for i in range(8, rows, 8):
        t = t + v[i : i + 8]
    s = t[:, :128]
    for j in range(128, columns, 128):
        s = s + t[:, j : j + 128]
    return s


def fold_row(v):
    t = jnp.sum(v, axis=0, keepdims=True)
    s = t[:, :128]
    for j in range(128, v.shape[1], 128):
        s = s + t[:, j : j + 128]
    return s


def pairs_of(n):
    return [(i, j) for i in range(n) for j in range(i, n)]


def tree_weights(gram, n):
    if n == 1:
        return [None]
    half = n // 2

    def at(i, j):
        return gram[(min(i, j), max(i, j))]

    low, high = [], []
    for j in range(half):
        product = at(j, j + half)
        low.append(1.0 - product / (2.0 * (at(j, j) + EPSILON)))
        high.append(1.0 - product / (2.0 * (at(j + half, j + half) + EPSILON)))
    if half == 1:
        return low + high
    merged = {}
    for j, k in pairs_of(half):
        merged[(j, k)] = (
            low[j] * low[k] * at(j, k)
            + low[j] * high[k] * at(j, k + half)
            + high[j] * low[k] * at(j + half, k)
            + high[j] * high[k] * at(j + half, k + half)
        )
    outer = tree_weights(merged, half)
    return [outer[j] * low[j] for j in range(half)] + [outer[j] * high[j] for j in range(half)]


def scratch_of(n_x, n_y, rows, width, hidden):
    n_z = 2 * n_y
    quarter = rows // n_x
    half, part, own = width // 2, width // (2 * n_y), width // (2 * n_y * n_z)
    stat_y = -(-len(pairs_of(n_y)) // 8) * 8
    stat_z = -(-len(pairs_of(n_z)) // 8) * 8
    group = 2 * n_x
    dma = pltpu.SemaphoreType.DMA
    return {
        "w_in": pltpu.VMEM((width, hidden), BF16),
        "w_out": pltpu.VMEM((hidden, width), BF16),
        "x": pltpu.VMEM((rows, width), BF16),
        "target": pltpu.VMEM((quarter, width), BF16),
        "order": pltpu.VMEM((width, width), BF16),
        "x_t": pltpu.VMEM((width, rows), BF16),
        "err_t": pltpu.VMEM((width, rows), BF16),
        "hid": pltpu.VMEM((rows, hidden), BF16),
        "slope": pltpu.VMEM((rows, hidden), F32),
        "out_own": pltpu.VMEM((quarter, width), F32),
        "out_send": pltpu.VMEM((n_x - 1, quarter, width), BF16),
        "out_recv": pltpu.VMEM((n_x - 1, quarter, width), BF16),
        "err": pltpu.VMEM((rows, width), BF16),
        "dpre": pltpu.VMEM((rows, hidden), BF16),
        "keep": pltpu.VMEM((2, half, hidden), F32),
        "send": pltpu.VMEM((2, half, hidden), BF16),
        "recv": pltpu.VMEM((2, half, hidden), BF16),
        "node": pltpu.VMEM((2, half, hidden), BF16),
        "y_recv": pltpu.VMEM((n_y, 2, part, hidden), BF16),
        "y_merged": pltpu.VMEM((2, part, hidden), F32),
        "z_send": pltpu.VMEM((n_z, 2, own, hidden), BF16),
        "z_recv": pltpu.VMEM((n_z, 2, own, hidden), BF16),
        "a0": pltpu.VMEM((group, 24, 128), F32),
        "a1": pltpu.VMEM((group, stat_y, 128), F32),
        "b1": pltpu.VMEM((n_y, stat_y, 128), F32),
        "a2": pltpu.VMEM((group, stat_z, 128), F32),
        "b2": pltpu.VMEM((n_y, stat_z, 128), F32),
        "c2": pltpu.VMEM((n_z, stat_z, 128), F32),
        "local": dma((2,)),
        "perm_s": dma((3,)),
        "perm_r": dma((3,)),
        "x_s": dma((2, n_x)),
        "x_r": dma((2, n_x)),
        "out_s": dma((n_x,)),
        "out_r": dma((n_x,)),
        "err_s": dma((n_x,)),
        "err_r": dma((n_x,)),
        "core_s": dma((2,)),
        "core_r": dma((2,)),
        "y_s": dma((2, n_y)),
        "y_r": dma((2, n_y)),
        "z_s": dma((n_z,)),
        "z_r": dma((n_z,)),
        "a0_s": dma((group,)),
        "a0_r": dma((group,)),
        "a1_s": dma((group,)),
        "a1_r": dma((group,)),
        "b1_s": dma((n_y,)),
        "b1_r": dma((n_y,)),
        "a2_s": dma((group,)),
        "a2_r": dma((group,)),
        "b2_s": dma((n_y,)),
        "b2_r": dma((n_y,)),
        "c2_s": dma((n_z,)),
        "c2_r": dma((n_z,)),
    }


class Refs:
    pass


def kernel(n_x, n_y, names, x_hbm, target_hbm, w_in_hbm, w_out_hbm, first_out, second_out, *scratch):
    s = Refs()
    for name, ref in zip(names, scratch):
        setattr(s, name, ref)
    n_z = 2 * n_y
    rows, width = x_hbm.shape
    hidden = w_in_hbm.shape[1]
    quarter = rows // n_x
    half, part, own = width // 2, width // (2 * n_y), width // (2 * n_y * n_z)
    width_tile, hidden_tile = tile_of(width), tile_of(hidden)

    me = lax.axis_index("dp")
    x = lax.axis_index("tensor")
    c = lax.rem(me, 2)
    y = lax.rem(lax.div(me, 2), n_y)
    z = lax.div(me, 2 * n_y)

    def dev(z_, y_, c_, x_):
        return {"dp": (z_ * n_y + y_) * 2 + c_, "tensor": x_}

    target_dev = dev(c * n_y + y, lax.rem(lax.rem(z, n_y) + y, n_y), 1 - lax.div(z, n_y), x)
    from_core = lax.div(z, n_y)
    from_y = lax.rem(z, n_y)
    y_node = lax.rem(y - from_y + n_y, n_y)
    source_dev = dev((1 - c) * n_y + y_node, from_y, from_core, x)
    z_node = from_y * 2 + from_core

    def x_peer(k):
        return dev(z, y, c, lax.rem(x + k, n_x))

    def group_peer(k):
        return dev(z, y, lax.rem(c + k // n_x, 2), lax.rem(x + k % n_x, n_x))

    def y_peer(k):
        return dev(z, lax.rem(y + k, n_y), c, x)

    def z_peer(k):
        return dev(lax.rem(z + k, n_z), y, c, x)

    fetch_in = pltpu.make_async_copy(w_in_hbm, s.w_in, s.local.at[0])
    fetch_out = pltpu.make_async_copy(w_out_hbm, s.w_out, s.local.at[1])
    fetch_in.start()
    fetch_out.start()

    barrier = pltpu.get_barrier_semaphore()
    everyone = [target_dev, source_dev]
    everyone += [group_peer(k) for k in range(1, 2 * n_x)]
    everyone += [y_peer(k) for k in range(1, n_y)]
    everyone += [z_peer(k) for k in range(1, n_z)]
    for peer in everyone:
        pl.semaphore_signal(barrier, inc=1, device_id=peer, device_id_type=MESH)
    pl.semaphore_wait(barrier, len(everyone))

    sent = []

    def push(src, dst, send_sem, recv_sem, peer):
        copy = pltpu.make_async_remote_copy(
            src_ref=src,
            dst_ref=dst,
            send_sem=send_sem,
            recv_sem=recv_sem,
            device_id=peer,
            device_id_type=MESH,
        )
        copy.start()
        sent.append(copy)
        return copy

    cut = -(-quarter // 32) * 16
    pieces = [(0, cut), (cut, quarter - cut)]
    moved = []
    for p, (start, size) in enumerate(pieces):
        at = block(x * quarter + start, size, 16)
        moved.append(push(x_hbm.at[at], s.x.at[at], s.perm_s.at[p], s.perm_r.at[p], target_dev))
    moved.append(
        push(
            target_hbm.at[block(x * quarter, quarter, 16)],
            s.target,
            s.perm_s.at[2],
            s.perm_r.at[2],
            target_dev,
        )
    )

    order_rows = tile_of(width)

    @pl.loop(0, width // order_rows)
    def _(step):
        base = step * order_rows
        i = lax.broadcasted_iota(jnp.int32, (order_rows, 128), 0) + base
        core_part = (i >= half).astype(jnp.int32)
        i = i - core_part * half
        y_part = jnp.zeros_like(i)
        for k in range(1, n_y):
            y_part = y_part + (i >= k * part).astype(jnp.int32)
        i = i - y_part * part
        z_part = jnp.zeros_like(i)
        for k in range(1, n_z):
            z_part = z_part + (i >= k * own).astype(jnp.int32)
        i = i - z_part * own
        column = ((z_part * n_y + y_part) * 2 + core_part) * own + i
        lanes = lax.broadcasted_iota(jnp.int32, (order_rows, 128), 1)
        for j in range(0, width, 128):
            size = min(128, width - j)
            hot = jnp.where(column == lanes + j, 1.0, 0.0)
            s.order[block(base, order_rows, 16), j : j + size] = hot[:, :size].astype(BF16)

    gathered = [{}, {}]
    for p, (start, size) in enumerate(pieces):
        moved[p].wait_recv()
        at = block(x * quarter + start, size, 16)
        for k in range(1, n_x):
            gathered[p][k] = push(
                s.x.at[at], s.x.at[at], s.x_s.at[p, k], s.x_r.at[p, k], x_peer(k)
            )

    fetch_in.wait()
    fetch_out.wait()

    steps = [0] + sorted(range(1, n_x), key=lambda k: min(k, n_x - k))
    partials = {}
    for k in steps:
        r = lax.rem(x - k + n_x, n_x)
        at = block(r * quarter, quarter, 16)
        if k:
            for p in range(2):
                gathered[p][k].wait_recv()

        @pl.loop(0, hidden // hidden_tile)
        def _(j):
            cols = block(j * hidden_tile, hidden_tile, hidden_tile)
            v = jnp.dot(s.x[at, :], s.w_in[:, cols], preferred_element_type=F32)
            v2 = v * v
            t = jnp.tanh(GELU_A * (v + GELU_B * (v * v2)))
            s.hid[at, cols] = (0.5 * v * (1.0 + t)).astype(BF16)
            s.slope[at, cols] = 0.5 * (1.0 + t) + (0.5 * v) * (1.0 - t * t) * (
                GELU_A * (1.0 + (3.0 * GELU_B) * v2)
            )

        @pl.loop(0, width // width_tile)
        def _(j):
            cols = block(j * width_tile, width_tile, width_tile)
            o = jnp.dot(s.hid[at, :], s.w_out[:, cols], preferred_element_type=F32)
            if k == 0:
                s.out_own[:, cols] = o
            else:
                s.out_send[k - 1, :, cols] = o.astype(BF16)

        if k:
            partials[k] = push(
                s.out_send.at[k - 1],
                s.out_recv.at[k - 1],
                s.out_s.at[k],
                s.out_r.at[k],
                dev(z, y, c, r),
            )

    @pl.loop(0, width // order_rows)
    def _(step):
        at = block(step * order_rows, order_rows, 16)
        s.x_t[at, :] = lax.dot_general(
            s.order[at, :], s.x[...], BY_ROWS, preferred_element_type=F32
        ).astype(BF16)

    moved[2].wait_recv()
    for k in steps[1:]:
        partials[k].wait_recv()

    @pl.loop(0, quarter // 16)
    def _(i):
        at = block(i * 16, 16, 16)
        total = s.out_own[at, :]
        for k in range(1, n_x):
            total = total + s.out_recv[k - 1, at, :].astype(F32)
        error = (total - s.target[at, :].astype(F32)) / rows
        s.err[block(x * quarter + i * 16, 16, 16), :] = error.astype(BF16)

    errors = {}
    mine = block(x * quarter, quarter, 16)
    for k in range(1, n_x):
        errors[k] = push(
            s.err.at[mine], s.err.at[mine], s.err_s.at[k], s.err_r.at[k], x_peer(k)
        )
    for k in steps:
        r = lax.rem(x - k + n_x, n_x)
        at = block(r * quarter, quarter, 16)
        if k:
            errors[k].wait_recv()

        @pl.loop(0, hidden // hidden_tile)
        def _(j):
            cols = block(j * hidden_tile, hidden_tile, hidden_tile)
            back = lax.dot_general(
                s.err[at, :], s.w_out[cols, :], BY_ROWS, preferred_element_type=F32
            )
            s.dpre[at, cols] = (back * s.slope[at, cols]).astype(BF16)

    mine = block(c * half, half, 16)
    theirs = block((1 - c) * half, half, 16)
    partner = dev(z, y, 1 - c, x)
    crossed = []
    for m, (left, right) in enumerate(((s.x_t, s.dpre), (s.err_t, s.hid))):
        if m == 1:

            @pl.loop(0, width // order_rows)
            def _(step):
                at = block(step * order_rows, order_rows, 16)
                s.err_t[at, :] = lax.dot_general(
                    s.order[at, :], s.err[...], BY_ROWS, preferred_element_type=F32
                ).astype(BF16)

        @pl.loop(0, hidden // hidden_tile)
        def _(j):
            cols = block(j * hidden_tile, hidden_tile, hidden_tile)
            s.send[m, :, cols] = jnp.dot(
                left[theirs, :], right[:, cols], preferred_element_type=F32
            ).astype(BF16)

        crossed.append(push(s.send.at[m], s.recv.at[m], s.core_s.at[m], s.core_r.at[m], partner))

        @pl.loop(0, hidden // hidden_tile)
        def _(j):
            cols = block(j * hidden_tile, hidden_tile, hidden_tile)
            s.keep[m, :, cols] = jnp.dot(
                left[mine, :], right[:, cols], preferred_element_type=F32
            )

    def total_over(buffer, send_sem, recv_sem, peer_of, count):
        copies = [
            push(buffer.at[0], buffer.at[k], send_sem.at[k], recv_sem.at[k], peer_of(k))
            for k in range(1, count)
        ]
        for copy in copies:
            copy.wait_recv()
        total = buffer[0]
        for k in range(1, count):
            total = total + buffer[k]
        return total

    stats = (jnp.zeros((8, 128), F32),) * 3
    for m in range(2):
        crossed[m].wait_recv()

        def level_sums(i, carry):
            at = block(i * 16, 16, 16)
            a = s.keep[m, at, :]
            b = s.recv[m, at, :].astype(F32)
            return (carry[0] + fold(a * b), carry[1] + fold(a * a), carry[2] + fold(b * b))

        stats = lax.fori_loop(0, half // 16, level_sums, stats)
    is_low = c == 1
    s.a0[0, 0:8, :] = stats[0]
    s.a0[0, 8:16, :] = jnp.where(is_low, stats[1], stats[2])
    s.a0[0, 16:24, :] = jnp.where(is_low, stats[2], stats[1])
    total = total_over(s.a0, s.a0_s, s.a0_r, group_peer, 2 * n_x)
    product, norm_low, norm_high = (
        jnp.sum(total[i * 8 : i * 8 + 8], keepdims=True) for i in range(3)
    )
    weights = tree_weights({(0, 0): norm_low, (0, 1): product, (1, 1): norm_high}, 2)
    weight_own = jnp.where(is_low, weights[0], weights[1])
    weight_other = jnp.where(is_low, weights[1], weights[0])

    y_copies = []
    for k in list(range(1, n_y)) + [0]:
        part_at = lax.rem(y + k, n_y) * part

        @pl.loop(0, part // 16)
        def _(i):
            at = block(part_at + i * 16, 16, 16)
            for m in range(2):
                node = weight_own * s.keep[m, at, :] + weight_other * s.recv[m, at, :].astype(F32)
                node = node.astype(BF16)
                if k:
                    s.node[m, at, :] = node
                else:
                    s.y_recv[y_node, m, block(i * 16, 16, 16), :] = node

        if k:
            for m in range(2):
                y_copies.append(
                    push(
                        s.node.at[m, block(part_at, part, 16)],
                        s.y_recv.at[y_node, m],
                        s.y_s.at[m, k],
                        s.y_r.at[m, k],
                        y_peer(k),
                    )
                )
    for copy in y_copies:
        copy.wait_recv()

    y_pairs = pairs_of(n_y)

    def y_sums(i, carry):
        at = block(i * 16, 16, 16)
        for m in range(2):
            nodes = [s.y_recv[j, m, at, :].astype(F32) for j in range(n_y)]
            carry = tuple(
                old + fold(nodes[a] * nodes[b]) for old, (a, b) in zip(carry, y_pairs)
            )
        return carry

    stats = lax.fori_loop(0, part // 16, y_sums, (jnp.zeros((8, 128), F32),) * len(y_pairs))
    s.a1[0] = jnp.zeros(s.a1.shape[1:], F32)
    for i, value in enumerate(stats):
        s.a1[0, i : i + 1, :] = jnp.sum(value, axis=0, keepdims=True)
    s.b1[0] = total_over(s.a1, s.a1_s, s.a1_r, group_peer, 2 * n_x)
    total = total_over(s.b1, s.b1_s, s.b1_r, y_peer, n_y)
    total = jnp.sum(total, axis=1, keepdims=True)
    weights = tree_weights({pair: total[i : i + 1] for i, pair in enumerate(y_pairs)}, n_y)

    @pl.loop(0, part // 16)
    def _(i):
        at = block(i * 16, 16, 16)
        for m in range(2):
            merged = weights[0] * s.y_recv[0, m, at, :].astype(F32)
            for j in range(1, n_y):
                merged = merged + weights[j] * s.y_recv[j, m, at, :].astype(F32)
            s.y_merged[m, at, :] = merged

    for j in range(n_z):
        for m in range(2):
            s.z_send[j, m] = s.y_merged[m, j * own : (j + 1) * own, :].astype(BF16)

    z_copies = []
    for k in range(1, n_z):
        z_copies.append(
            push(
                s.z_send.at[lax.rem(z + k, n_z)],
                s.z_recv.at[z_node],
                s.z_s.at[k],
                s.z_r.at[k],
                z_peer(k),
            )
        )
    s.z_recv[z_node] = s.z_send[z]
    for copy in z_copies:
        copy.wait_recv()

    z_pairs = pairs_of(n_z)
    s.a2[0] = jnp.zeros(s.a2.shape[1:], F32)
    for i, (a, b) in enumerate(z_pairs):
        value = 0.0
        for m in range(2):
            value = value + s.z_recv[a, m].astype(F32) * s.z_recv[b, m].astype(F32)
        s.a2[0, i : i + 1, :] = fold_row(value)
    s.b2[0] = total_over(s.a2, s.a2_s, s.a2_r, group_peer, 2 * n_x)
    s.c2[0] = total_over(s.b2, s.b2_s, s.b2_r, y_peer, n_y)
    total = total_over(s.c2, s.c2_s, s.c2_r, z_peer, n_z)
    total = jnp.sum(total, axis=1, keepdims=True)
    weights = tree_weights({pair: total[i : i + 1] for i, pair in enumerate(z_pairs)}, n_z)
    for m, out in enumerate((first_out, second_out)):
        merged = weights[0] * s.z_recv[0, m].astype(F32)
        for j in range(1, n_z):
            merged = merged + weights[j] * s.z_recv[j, m].astype(F32)
        out[...] = merged
    for copy in sent:
        copy.wait_send()


def solution(mesh):
    n_x = mesh.shape["tensor"]
    n_y = math.isqrt(mesh.shape["dp"] // 4)

    def on_device(inputs, targets, w_in, w_out):
        rows, width = inputs.shape
        hidden = w_in.shape[1]
        scratch = scratch_of(n_x, n_y, rows, width, hidden)
        share = jax.ShapeDtypeStruct((width // mesh.shape["dp"], hidden), F32)
        return pl.pallas_call(
            functools.partial(kernel, n_x, n_y, tuple(scratch)),
            out_shape=(share, share),
            in_specs=[pl.BlockSpec(memory_space=pl.ANY)] * 4,
            out_specs=(pl.BlockSpec(memory_space=pltpu.VMEM),) * 2,
            scratch_shapes=list(scratch.values()),
            compiler_params=pltpu.CompilerParams(
                collective_id=0, has_side_effects=True, vmem_limit_bytes=67_000_000
            ),
        )(inputs, targets, w_in, w_out)

    placed = (P("dp", None), P("dp", None), P(None, "tensor"), P("tensor", None))
    return jax.shard_map(
        on_device,
        mesh=mesh,
        in_specs=placed,
        out_specs=(P("dp", "tensor"), P("dp", "tensor")),
        check_vma=False,
    )
```

```python
import functools
import math

import jax
import jax.numpy as jnp
from jax import lax
from jax.experimental import pallas as pl
from jax.experimental.pallas import tpu as pltpu
from jax.sharding import PartitionSpec as P

F32, BF16 = jnp.float32, jnp.bfloat16
EPSILON = 1e-06
GELU_A = math.sqrt(2.0 / math.pi)
GELU_B = 0.044715
MESH = pl.DeviceIdType.MESH
BY_ROWS = (((1,), (1,)), ((), ()))


def tile_of(n):
    return 256 if n % 256 == 0 else n


def block(start, size, step):
    return pl.ds(pl.multiple_of(start, step), size)


def fold(v):
    rows, columns = v.shape
    t = v[0:8]
    for i in range(8, rows, 8):
        t = t + v[i : i + 8]
    s = t[:, :128]
    for j in range(128, columns, 128):
        s = s + t[:, j : j + 128]
    return s


def fold_row(v):
    t = jnp.sum(v, axis=0, keepdims=True)
    s = t[:, :128]
    for j in range(128, v.shape[1], 128):
        s = s + t[:, j : j + 128]
    return s


def pieces_of(rows):
    units, pieces = rows // 16, []
    for p in range(4):
        start = p * units // 4
        pieces.append((start * 16, ((p + 1) * units // 4 - start) * 16))
    return pieces


def pairs_of(n):
    return [(i, j) for i in range(n) for j in range(i, n)]


def tree_weights(gram, n):
    if n == 1:
        return [None]
    half = n // 2

    def at(i, j):
        return gram[(min(i, j), max(i, j))]

    low, high = [], []
    for j in range(half):
        product = at(j, j + half)
        low.append(1.0 - product / (2.0 * (at(j, j) + EPSILON)))
        high.append(1.0 - product / (2.0 * (at(j + half, j + half) + EPSILON)))
    if half == 1:
        return low + high
    merged = {}
    for j, k in pairs_of(half):
        merged[(j, k)] = (
            low[j] * low[k] * at(j, k)
            + low[j] * high[k] * at(j, k + half)
            + high[j] * low[k] * at(j + half, k)
            + high[j] * high[k] * at(j + half, k + half)
        )
    outer = tree_weights(merged, half)
    return [outer[j] * low[j] for j in range(half)] + [outer[j] * high[j] for j in range(half)]


def scratch_of(n_x, n_y, rows, width, hidden):
    n_z = 2 * n_y
    quarter = rows // n_x
    half, part, own = width // 2, width // (2 * n_y), width // (2 * n_y * n_z)
    stat_y = -(-len(pairs_of(n_y)) // 8) * 8
    stat_z = -(-len(pairs_of(n_z)) // 8) * 8
    group = 2 * n_x
    dma = pltpu.SemaphoreType.DMA
    return {
        "w_in": pltpu.VMEM((width, hidden), BF16),
        "w_out": pltpu.VMEM((hidden, width), BF16),
        "x": pltpu.VMEM((rows, width), BF16),
        "target": pltpu.VMEM((quarter, width), BF16),
        "order": pltpu.VMEM((width, width), BF16),
        "x_t": pltpu.VMEM((width, rows), BF16),
        "err_t": pltpu.VMEM((n_x, width, quarter), BF16),
        "hid": pltpu.VMEM((rows, hidden), BF16),
        "slope": pltpu.VMEM((rows, hidden), F32),
        "out_own": pltpu.VMEM((quarter, width), F32),
        "out_send": pltpu.VMEM((n_x - 1, quarter, width), BF16),
        "out_recv": pltpu.VMEM((n_x - 1, quarter, width), BF16),
        "err": pltpu.VMEM((rows, width), BF16),
        "dpre": pltpu.VMEM((rows, hidden), BF16),
        "keep": pltpu.VMEM((half, hidden), F32),
        "second": pltpu.VMEM((width, hidden), F32),
        "send": pltpu.VMEM((2, half, hidden), BF16),
        "recv": pltpu.VMEM((2, half, hidden), BF16),
        "node": pltpu.VMEM((2, half, hidden), BF16),
        "y_recv": pltpu.VMEM((n_y, 2, part, hidden), BF16),
        "y_merged": pltpu.VMEM((2, part, hidden), F32),
        "z_send": pltpu.VMEM((n_z, 2, own, hidden), BF16),
        "z_recv": pltpu.VMEM((n_z, 2, own, hidden), BF16),
        "a0": pltpu.VMEM((group, 24, 128), F32),
        "a1": pltpu.VMEM((group, stat_y, 128), F32),
        "b1": pltpu.VMEM((n_y, stat_y, 128), F32),
        "a2": pltpu.VMEM((group, stat_z, 128), F32),
        "b2": pltpu.VMEM((n_y, stat_z, 128), F32),
        "c2": pltpu.VMEM((n_z, stat_z, 128), F32),
        "local": dma((2,)),
        "relay": pltpu.VMEM((quarter, width), BF16),
        "target_relay": pltpu.VMEM((quarter, width), BF16),
        "hop1_s": dma((5,)),
        "hop1_r": dma((5,)),
        "hop2_s": dma((5,)),
        "hop2_r": dma((5,)),
        "x_s": dma((4, n_x)),
        "x_r": dma((4, n_x)),
        "out_s": dma((n_x,)),
        "out_r": dma((n_x,)),
        "err_s": dma((4, n_x)),
        "err_r": dma((4, n_x)),
        "core_s": dma((2,)),
        "core_r": dma((2,)),
        "y_s": dma((2, n_y)),
        "y_r": dma((2, n_y)),
        "z_s": dma((n_z,)),
        "z_r": dma((n_z,)),
        "a0_s": dma((group,)),
        "a0_r": dma((group,)),
        "a1_s": dma((group,)),
        "a1_r": dma((group,)),
        "b1_s": dma((n_y,)),
        "b1_r": dma((n_y,)),
        "a2_s": dma((group,)),
        "a2_r": dma((group,)),
        "b2_s": dma((n_y,)),
        "b2_r": dma((n_y,)),
        "c2_s": dma((n_z,)),
        "c2_r": dma((n_z,)),
    }


class Refs:
    pass


def kernel(n_x, n_y, names, x_hbm, target_hbm, w_in_hbm, w_out_hbm, first_out, second_out, *scratch):
    s = Refs()
    for name, ref in zip(names, scratch):
        setattr(s, name, ref)
    n_z = 2 * n_y
    rows, width = x_hbm.shape
    hidden = w_in_hbm.shape[1]
    quarter = rows // n_x
    half, part, own = width // 2, width // (2 * n_y), width // (2 * n_y * n_z)
    width_tile, hidden_tile = tile_of(width), tile_of(hidden)

    me = lax.axis_index("dp")
    x = lax.axis_index("tensor")
    c = lax.rem(me, 2)
    y = lax.rem(lax.div(me, 2), n_y)
    z = lax.div(me, 2 * n_y)

    def dev(z_, y_, c_, x_):
        return {"dp": (z_ * n_y + y_) * 2 + c_, "tensor": x_}

    z_low = lax.rem(z, n_y)
    relay_dev = dev(z, lax.rem(y + z_low, n_y), 1 - c, x)
    relayed_y = lax.rem(y - z_low + n_y, n_y)
    relayed_dev = dev(z, relayed_y, 1 - c, x)
    final_dev = dev((1 - c) * n_y + relayed_y, y, lax.div(z, n_y), x)
    from_core = lax.div(z, n_y)
    from_y = lax.rem(z, n_y)
    y_node = lax.rem(y - from_y + n_y, n_y)
    source_dev = dev(c * n_y + y_node, y, 1 - from_core, x)
    z_node = from_y * 2 + from_core

    def x_peer(k):
        return dev(z, y, c, lax.rem(x + k, n_x))

    def group_peer(k):
        return dev(z, y, lax.rem(c + k // n_x, 2), lax.rem(x + k % n_x, n_x))

    def y_peer(k):
        return dev(z, lax.rem(y + k, n_y), c, x)

    def z_peer(k):
        return dev(lax.rem(z + k, n_z), y, c, x)

    fetch_in = pltpu.make_async_copy(w_in_hbm, s.w_in, s.local.at[0])
    fetch_out = pltpu.make_async_copy(w_out_hbm, s.w_out, s.local.at[1])
    fetch_in.start()
    fetch_out.start()

    barrier = pltpu.get_barrier_semaphore()
    everyone = [relay_dev, relayed_dev, final_dev, source_dev]
    everyone += [group_peer(k) for k in range(1, 2 * n_x)]
    everyone += [y_peer(k) for k in range(1, n_y)]
    everyone += [z_peer(k) for k in range(1, n_z)]
    for peer in everyone:
        pl.semaphore_signal(barrier, inc=1, device_id=peer, device_id_type=MESH)
    pl.semaphore_wait(barrier, len(everyone))

    sent = []

    def push(src, dst, send_sem, recv_sem, peer):
        copy = pltpu.make_async_remote_copy(
            src_ref=src,
            dst_ref=dst,
            send_sem=send_sem,
            recv_sem=recv_sem,
            device_id=peer,
            device_id_type=MESH,
        )
        copy.start()
        sent.append(copy)
        return copy

    pieces = pieces_of(quarter)
    share = block(x * quarter, quarter, 16)
    x_from, target_from = x_hbm.at[share], target_hbm.at[share]
    hops = []
    for p, (start, size) in enumerate(pieces):
        at = pl.ds(start, size)
        hops.append(
            push(x_from.at[at], s.relay.at[at], s.hop1_s.at[p], s.hop1_r.at[p], relay_dev)
        )
    moved = []
    for p, (start, size) in enumerate(pieces):
        hops[p].wait_recv()
        moved.append(
            push(
                s.relay.at[pl.ds(start, size)],
                s.x.at[block(x * quarter + start, size, 16)],
                s.hop2_s.at[p],
                s.hop2_r.at[p],
                final_dev,
            )
        )
    last_piece = len(pieces)
    hops.append(
        push(
            target_from,
            s.target_relay,
            s.hop1_s.at[last_piece],
            s.hop1_r.at[last_piece],
            relay_dev,
        )
    )

    near = sorted({1, n_x - 1})
    relays = [(p, near[p * len(near) // len(pieces)]) for p in (0, 2, 1, 3)]

    def rows_of(k, p):
        start, size = pieces[p]
        return block(lax.rem(x - k + n_x, n_x) * quarter + start, size, 16)

    def give(ref, p, send_sem, recv_sem):
        at = rows_of(0, p)
        return {
            (k, p): push(ref.at[at], ref.at[at], send_sem.at[p, k], recv_sem.at[p, k], x_peer(k))
            for k in near
        }

    def relay(ref, given, send_sem, recv_sem):
        if n_x == 4:
            for p, k in relays:
                given[(k, p)].wait_recv()
                at = rows_of(k, p)
                given[(2, p)] = push(
                    ref.at[at], ref.at[at], send_sem.at[p, 2], recv_sem.at[p, 2], x_peer(k)
                )

    def take(given, k):
        for p in range(len(pieces)):
            if n_x < 4 or (p, k) not in relays:
                given[(k, p)].wait_recv()

    given = {}
    for p in range(len(pieces)):
        moved[p].wait_recv()
        given.update(give(s.x, p, s.x_s, s.x_r))

    fetch_in.wait()
    fetch_out.wait()

    steps = [0] + sorted(range(1, n_x), key=lambda k: min(k, n_x - k))
    partials = {}
    for k in steps:
        r = lax.rem(x - k + n_x, n_x)
        at = block(r * quarter, quarter, 16)
        if k == 1:
            relay(s.x, given, s.x_s, s.x_r)
            hops[last_piece].wait_recv()
            moved.append(
                push(
                    s.target_relay,
                    s.target,
                    s.hop2_s.at[last_piece],
                    s.hop2_r.at[last_piece],
                    final_dev,
                )
            )
        if k:
            take(given, k)

        @pl.loop(0, hidden // hidden_tile)
        def _(j):
            cols = block(j * hidden_tile, hidden_tile, hidden_tile)
            v = jnp.dot(s.x[at, :], s.w_in[:, cols], preferred_element_type=F32)
            v2 = v * v
            t = jnp.tanh(GELU_A * (v + GELU_B * (v * v2)))
            s.hid[at, cols] = (0.5 * v * (1.0 + t)).astype(BF16)
            s.slope[at, cols] = 0.5 * (1.0 + t) + (0.5 * v) * (1.0 - t * t) * (
                GELU_A * (1.0 + (3.0 * GELU_B) * v2)
            )

        @pl.loop(0, width // width_tile)
        def _(j):
            cols = block(j * width_tile, width_tile, width_tile)
            o = jnp.dot(s.hid[at, :], s.w_out[:, cols], preferred_element_type=F32)
            if k == 0:
                s.out_own[:, cols] = o
            else:
                s.out_send[k - 1, :, cols] = o.astype(BF16)

        if k:
            partials[k] = push(
                s.out_send.at[k - 1],
                s.out_recv.at[k - 1],
                s.out_s.at[k],
                s.out_r.at[k],
                dev(z, y, c, r),
            )

    order_rows = tile_of(width)

    @pl.loop(0, width // order_rows)
    def _(step):
        base = step * order_rows
        i = lax.broadcasted_iota(jnp.int32, (order_rows, 128), 0) + base
        core_part = (i >= half).astype(jnp.int32)
        i = i - core_part * half
        y_part = jnp.zeros_like(i)
        for k in range(1, n_y):
            y_part = y_part + (i >= k * part).astype(jnp.int32)
        i = i - y_part * part
        z_part = jnp.zeros_like(i)
        for k in range(1, n_z):
            z_part = z_part + (i >= k * own).astype(jnp.int32)
        i = i - z_part * own
        column = ((z_part * n_y + y_part) * 2 + core_part) * own + i
        lanes = lax.broadcasted_iota(jnp.int32, (order_rows, 128), 1)
        for j in range(0, width, 128):
            size = min(128, width - j)
            hot = jnp.where(column == lanes + j, 1.0, 0.0)
            s.order[block(base, order_rows, 16), j : j + size] = hot[:, :size].astype(BF16)

    @pl.loop(0, width // order_rows)
    def _(step):
        at = block(step * order_rows, order_rows, 16)
        s.x_t[at, :] = lax.dot_general(
            s.order[at, :], s.x[...], BY_ROWS, preferred_element_type=F32
        ).astype(BF16)

    moved[last_piece].wait_recv()
    for k in steps[1:]:
        partials[k].wait_recv()

    @pl.loop(0, quarter // 16)
    def _(i):
        at = block(i * 16, 16, 16)
        total = s.out_own[at, :]
        for k in range(1, n_x):
            total = total + s.out_recv[k - 1, at, :].astype(F32)
        error = (total - s.target[at, :].astype(F32)) / rows
        s.err[block(x * quarter + i * 16, 16, 16), :] = error.astype(BF16)

    given = {}
    for p in range(len(pieces)):
        given.update(give(s.err, p, s.err_s, s.err_r))
    mine = block(c * half, half, 16)
    theirs = block((1 - c) * half, half, 16)
    partner = dev(z, y, 1 - c, x)
    crossed = []

    def cross(m):
        crossed.append(push(s.send.at[m], s.recv.at[m], s.core_s.at[m], s.core_r.at[m], partner))

    def gradient_first(at, store):
        @pl.loop(0, hidden // hidden_tile)
        def _(j):
            cols = block(j * hidden_tile, hidden_tile, hidden_tile)
            store(cols, jnp.dot(s.x_t[at, :], s.dpre[:, cols], preferred_element_type=F32))

    def store_send(cols, value):
        s.send[0, :, cols] = value.astype(BF16)

    def store_keep(cols, value):
        s.keep[:, cols] = value

    for turn, k in enumerate(steps):
        r = lax.rem(x - k + n_x, n_x)
        at = block(r * quarter, quarter, 16)
        if k == 1:
            relay(s.err, given, s.err_s, s.err_r)
        if k:
            take(given, k)

        @pl.loop(0, hidden // hidden_tile)
        def _(j):
            cols = block(j * hidden_tile, hidden_tile, hidden_tile)
            back = lax.dot_general(
                s.err[at, :], s.w_out[cols, :], BY_ROWS, preferred_element_type=F32
            )
            s.dpre[at, cols] = (back * s.slope[at, cols]).astype(BF16)

        last = turn == len(steps) - 1
        if last:
            gradient_first(theirs, store_send)
            cross(0)

        @pl.loop(0, width // order_rows)
        def _(step):
            some = block(step * order_rows, order_rows, 16)
            s.err_t[k, some, :] = lax.dot_general(
                s.order[some, :], s.err[at, :], BY_ROWS, preferred_element_type=F32
            ).astype(BF16)

        @pl.loop(0, hidden // hidden_tile)
        def _(j):
            cols = block(j * hidden_tile, hidden_tile, hidden_tile)
            if last:
                s.send[1, :, cols] = (
                    s.second[theirs, cols]
                    + jnp.dot(s.err_t[k, theirs, :], s.hid[at, cols], preferred_element_type=F32)
                ).astype(BF16)
                s.second[mine, cols] += jnp.dot(
                    s.err_t[k, mine, :], s.hid[at, cols], preferred_element_type=F32
                )
            else:
                value = jnp.dot(s.err_t[k], s.hid[at, cols], preferred_element_type=F32)
                if turn == 0:
                    s.second[:, cols] = value
                else:
                    s.second[:, cols] += value

        if last:
            cross(1)
            gradient_first(mine, store_keep)

    def own_part(m, start):
        if m == 0:
            return s.keep[block(start, 16, 16), :]
        return s.second[block(c * half + start, 16, 16), :]

    def total_over(buffer, send_sem, recv_sem, peer_of, count):
        copies = [
            push(buffer.at[0], buffer.at[k], send_sem.at[k], recv_sem.at[k], peer_of(k))
            for k in range(1, count)
        ]
        for copy in copies:
            copy.wait_recv()
        total = buffer[0]
        for k in range(1, count):
            total = total + buffer[k]
        return total

    stats = (jnp.zeros((8, 128), F32),) * 3
    for m in range(2):
        crossed[m].wait_recv()

        def level_sums(i, carry):
            at = block(i * 16, 16, 16)
            a = own_part(m, i * 16)
            b = s.recv[m, at, :].astype(F32)
            return (carry[0] + fold(a * b), carry[1] + fold(a * a), carry[2] + fold(b * b))

        stats = lax.fori_loop(0, half // 16, level_sums, stats)
    is_low = c == 0
    s.a0[0, 0:8, :] = stats[0]
    s.a0[0, 8:16, :] = jnp.where(is_low, stats[1], stats[2])
    s.a0[0, 16:24, :] = jnp.where(is_low, stats[2], stats[1])
    total = total_over(s.a0, s.a0_s, s.a0_r, group_peer, 2 * n_x)
    product, norm_low, norm_high = (
        jnp.sum(total[i * 8 : i * 8 + 8], keepdims=True) for i in range(3)
    )
    weights = tree_weights({(0, 0): norm_low, (0, 1): product, (1, 1): norm_high}, 2)
    weight_own = jnp.where(is_low, weights[0], weights[1])
    weight_other = jnp.where(is_low, weights[1], weights[0])

    y_copies = []
    for k in list(range(1, n_y)) + [0]:
        part_at = lax.rem(y + k, n_y) * part

        @pl.loop(0, part // 16)
        def _(i):
            at = block(part_at + i * 16, 16, 16)
            for m in range(2):
                node = weight_own * own_part(m, part_at + i * 16)
                node = node + weight_other * s.recv[m, at, :].astype(F32)
                node = node.astype(BF16)
                if k:
                    s.node[m, at, :] = node
                else:
                    s.y_recv[y_node, m, block(i * 16, 16, 16), :] = node

        if k:
            for m in range(2):
                y_copies.append(
                    push(
                        s.node.at[m, block(part_at, part, 16)],
                        s.y_recv.at[y_node, m],
                        s.y_s.at[m, k],
                        s.y_r.at[m, k],
                        y_peer(k),
                    )
                )
    for copy in y_copies:
        copy.wait_recv()

    y_pairs = pairs_of(n_y)

    def y_sums(i, carry):
        at = block(i * 16, 16, 16)
        for m in range(2):
            nodes = [s.y_recv[j, m, at, :].astype(F32) for j in range(n_y)]
            carry = tuple(
                old + fold(nodes[a] * nodes[b]) for old, (a, b) in zip(carry, y_pairs)
            )
        return carry

    stats = lax.fori_loop(0, part // 16, y_sums, (jnp.zeros((8, 128), F32),) * len(y_pairs))
    s.a1[0] = jnp.zeros(s.a1.shape[1:], F32)
    for i, value in enumerate(stats):
        s.a1[0, i : i + 1, :] = jnp.sum(value, axis=0, keepdims=True)
    s.b1[0] = total_over(s.a1, s.a1_s, s.a1_r, group_peer, 2 * n_x)
    total = total_over(s.b1, s.b1_s, s.b1_r, y_peer, n_y)
    total = jnp.sum(total, axis=1, keepdims=True)
    weights = tree_weights({pair: total[i : i + 1] for i, pair in enumerate(y_pairs)}, n_y)

    @pl.loop(0, part // 16)
    def _(i):
        at = block(i * 16, 16, 16)
        for m in range(2):
            merged = weights[0] * s.y_recv[0, m, at, :].astype(F32)
            for j in range(1, n_y):
                merged = merged + weights[j] * s.y_recv[j, m, at, :].astype(F32)
            s.y_merged[m, at, :] = merged

    for j in range(n_z):
        for m in range(2):
            s.z_send[j, m] = s.y_merged[m, j * own : (j + 1) * own, :].astype(BF16)

    z_copies = []
    for k in range(1, n_z):
        z_copies.append(
            push(
                s.z_send.at[lax.rem(z + k, n_z)],
                s.z_recv.at[z_node],
                s.z_s.at[k],
                s.z_r.at[k],
                z_peer(k),
            )
        )
    s.z_recv[z_node] = s.z_send[z]
    for copy in z_copies:
        copy.wait_recv()

    z_pairs = pairs_of(n_z)
    s.a2[0] = jnp.zeros(s.a2.shape[1:], F32)
    for i, (a, b) in enumerate(z_pairs):
        value = 0.0
        for m in range(2):
            value = value + s.z_recv[a, m].astype(F32) * s.z_recv[b, m].astype(F32)
        s.a2[0, i : i + 1, :] = fold_row(value)
    s.b2[0] = total_over(s.a2, s.a2_s, s.a2_r, group_peer, 2 * n_x)
    s.c2[0] = total_over(s.b2, s.b2_s, s.b2_r, y_peer, n_y)
    total = total_over(s.c2, s.c2_s, s.c2_r, z_peer, n_z)
    total = jnp.sum(total, axis=1, keepdims=True)
    weights = tree_weights({pair: total[i : i + 1] for i, pair in enumerate(z_pairs)}, n_z)
    for m, out in enumerate((first_out, second_out)):
        merged = weights[0] * s.z_recv[0, m].astype(F32)
        for j in range(1, n_z):
            merged = merged + weights[j] * s.z_recv[j, m].astype(F32)
        out[...] = merged
    for copy in sent:
        copy.wait_send()


def solution(mesh):
    n_x = mesh.shape["tensor"]
    n_y = math.isqrt(mesh.shape["dp"] // 4)

    def on_device(inputs, targets, w_in, w_out):
        rows, width = inputs.shape
        hidden = w_in.shape[1]
        scratch = scratch_of(n_x, n_y, rows, width, hidden)
        share = jax.ShapeDtypeStruct((width // mesh.shape["dp"], hidden), F32)
        return pl.pallas_call(
            functools.partial(kernel, n_x, n_y, tuple(scratch)),
            out_shape=(share, share),
            in_specs=[pl.BlockSpec(memory_space=pl.ANY)] * 4,
            out_specs=(pl.BlockSpec(memory_space=pltpu.VMEM),) * 2,
            scratch_shapes=list(scratch.values()),
            compiler_params=pltpu.CompilerParams(
                collective_id=0, has_side_effects=True, vmem_limit_bytes=67_000_000
            ),
        )(inputs, targets, w_in, w_out)

    placed = (P("dp", None), P("dp", None), P(None, "tensor"), P("tensor", None))
    return jax.shard_map(
        on_device,
        mesh=mesh,
        in_specs=placed,
        out_specs=(P("dp", "tensor"), P("dp", "tensor")),
        check_vma=False,
    )
```

```python
import functools
import math

import jax
import jax.numpy as jnp
from jax import lax
from jax.experimental import pallas as pl
from jax.experimental.pallas import tpu as pltpu
from jax.sharding import PartitionSpec as P

F32, BF16 = jnp.float32, jnp.bfloat16
EPSILON = 1e-06
GELU_A = math.sqrt(2.0 / math.pi)
GELU_B = 0.044715
MESH = pl.DeviceIdType.MESH
BY_ROWS = (((1,), (1,)), ((), ()))


def tile_of(n):
    return 256 if n % 256 == 0 else n


def block(start, size, step):
    return pl.ds(pl.multiple_of(start, step), size)


def fold(v):
    rows, columns = v.shape
    t = v[0:8]
    for i in range(8, rows, 8):
        t = t + v[i : i + 8]
    s = t[:, :128]
    for j in range(128, columns, 128):
        s = s + t[:, j : j + 128]
    return s


def fold_row(v):
    t = jnp.sum(v, axis=0, keepdims=True)
    s = t[:, :128]
    for j in range(128, v.shape[1], 128):
        s = s + t[:, j : j + 128]
    return s


def pieces_of(rows):
    units, pieces = rows // 16, []
    for p in range(4):
        start = p * units // 4
        pieces.append((start * 16, ((p + 1) * units // 4 - start) * 16))
    return pieces


def diagonal(n):
    shape = (n, 128)
    return lax.broadcasted_iota(jnp.int32, shape, 0) == lax.broadcasted_iota(jnp.int32, shape, 1)


def pack(rows, values):
    rows[...] = jnp.zeros(rows.shape, F32)
    for i, value in enumerate(values):
        rows[i : i + 1, :] = jnp.sum(value, axis=0, keepdims=True)
    column = jnp.sum(rows[...], axis=1, keepdims=True)
    line = jnp.sum(jnp.where(diagonal(rows.shape[0]), column, 0.0), axis=0, keepdims=True)
    return jnp.broadcast_to(line, (8, 128))


def unpack(total, names, n):
    line = jnp.broadcast_to(total[0:1], (n, 128))
    column = jnp.sum(jnp.where(diagonal(n), line, 0.0), axis=1, keepdims=True)
    return {name: column[i : i + 1] for i, name in enumerate(names)}


def pairs_of(n):
    return [(i, j) for i in range(n) for j in range(i, n)]


def tree_weights(gram, n):
    if n == 1:
        return [None]
    half = n // 2

    def at(i, j):
        return gram[(min(i, j), max(i, j))]

    low, high = [], []
    for j in range(half):
        product = at(j, j + half)
        low.append(1.0 - product / (2.0 * (at(j, j) + EPSILON)))
        high.append(1.0 - product / (2.0 * (at(j + half, j + half) + EPSILON)))
    if half == 1:
        return low + high
    merged = {}
    for j, k in pairs_of(half):
        merged[(j, k)] = (
            low[j] * low[k] * at(j, k)
            + low[j] * high[k] * at(j, k + half)
            + high[j] * low[k] * at(j + half, k)
            + high[j] * high[k] * at(j + half, k + half)
        )
    outer = tree_weights(merged, half)
    return [outer[j] * low[j] for j in range(half)] + [outer[j] * high[j] for j in range(half)]


def scratch_of(n_x, n_y, rows, width, hidden):
    n_z = 2 * n_y
    quarter = rows // n_x
    half, part, own = width // 2, width // (2 * n_y), width // (2 * n_y * n_z)
    stat_y = -(-len(pairs_of(n_y)) // 8) * 8
    stat_z = -(-len(pairs_of(n_z)) // 8) * 8
    group = 2 * n_x
    tiles = width // tile_of(width)
    dma = pltpu.SemaphoreType.DMA
    return {
        "w_in": pltpu.VMEM((width, hidden), BF16),
        "w_out": pltpu.VMEM((hidden, width), BF16),
        "w_back": pltpu.VMEM((hidden, width), BF16),
        "target_back": pltpu.VMEM((quarter, width), BF16),
        "x": pltpu.VMEM((rows, width), BF16),
        "target": pltpu.VMEM((quarter, width), BF16),
        "order": pltpu.VMEM((width, width), BF16),
        "x_t": pltpu.VMEM((width, rows), BF16),
        "err_t": pltpu.VMEM((n_x, width, quarter), BF16),
        "hid": pltpu.VMEM((rows, hidden), BF16),
        "slope": pltpu.VMEM((rows, hidden), F32),
        "out_own": pltpu.VMEM((quarter, width), F32),
        "out_send": pltpu.VMEM((n_x - 1, tiles, quarter, width // tiles), BF16),
        "out_recv": pltpu.VMEM((n_x - 1, tiles, quarter, width // tiles), BF16),
        "err": pltpu.VMEM((rows, width), BF16),
        "dpre": pltpu.VMEM((rows, hidden), BF16),
        "keep": pltpu.VMEM((half, hidden), F32),
        "second": pltpu.VMEM((width, hidden), F32),
        "send": pltpu.VMEM((2, half, hidden), BF16),
        "recv": pltpu.VMEM((2, half, hidden), BF16),
        "node": pltpu.VMEM((2, half, hidden), BF16),
        "y_recv": pltpu.VMEM((n_y, 2, part, hidden), BF16),
        "y_merged": pltpu.VMEM((2, part, hidden), F32),
        "z_send": pltpu.VMEM((n_z, 2, own, hidden), BF16),
        "z_recv": pltpu.VMEM((n_z, 2, own, hidden), BF16),
        "r0": pltpu.VMEM((8, 128), F32),
        "r1": pltpu.VMEM((stat_y, 128), F32),
        "r2": pltpu.VMEM((stat_z, 128), F32),
        "a0": pltpu.VMEM((group, 8, 128), F32),
        "a1": pltpu.VMEM((group, 8, 128), F32),
        "b1": pltpu.VMEM((n_y, 8, 128), F32),
        "a2": pltpu.VMEM((group, 8, 128), F32),
        "b2": pltpu.VMEM((n_y, 8, 128), F32),
        "c2": pltpu.VMEM((n_z, 8, 128), F32),
        "local": dma((2,)),
        "relay": pltpu.VMEM((quarter, width), BF16),
        "target_relay": pltpu.VMEM((quarter, width), BF16),
        "hop1_s": dma((5,)),
        "hop1_r": dma((5,)),
        "hop2_s": dma((5,)),
        "hop2_r": dma((5,)),
        "x_s": dma((4, n_x)),
        "x_r": dma((4, n_x)),
        "out_s": dma((tiles, n_x)),
        "out_r": dma((tiles, n_x)),
        "err_s": dma((4, n_x)),
        "err_r": dma((4, n_x)),
        "core_s": dma((2,)),
        "core_r": dma((2,)),
        "y_s": dma((2, n_y)),
        "y_r": dma((2, n_y)),
        "z_s": dma((n_z,)),
        "z_r": dma((n_z,)),
        "a0_s": dma((group,)),
        "a0_r": dma((group,)),
        "a1_s": dma((group,)),
        "a1_r": dma((group,)),
        "b1_s": dma((n_y,)),
        "b1_r": dma((n_y,)),
        "a2_s": dma((group,)),
        "a2_r": dma((group,)),
        "b2_s": dma((n_y,)),
        "b2_r": dma((n_y,)),
        "c2_s": dma((n_z,)),
        "c2_r": dma((n_z,)),
    }


class Refs:
    pass


def kernel(n_x, n_y, names, x_hbm, target_hbm, w_in_hbm, w_out_hbm, first_out, second_out, *scratch):
    s = Refs()
    for name, ref in zip(names, scratch):
        setattr(s, name, ref)
    n_z = 2 * n_y
    rows, width = x_hbm.shape
    hidden = w_in_hbm.shape[1]
    quarter = rows // n_x
    half, part, own = width // 2, width // (2 * n_y), width // (2 * n_y * n_z)
    width_tile, hidden_tile = tile_of(width), tile_of(hidden)

    me = lax.axis_index("dp")
    x = lax.axis_index("tensor")
    c = lax.rem(me, 2)
    y = lax.rem(lax.div(me, 2), n_y)
    z = lax.div(me, 2 * n_y)

    def dev(z_, y_, c_, x_):
        return {"dp": (z_ * n_y + y_) * 2 + c_, "tensor": x_}

    z_low = lax.rem(z, n_y)
    relay_dev = dev(z, lax.rem(y + z_low, n_y), 1 - c, x)
    relayed_y = lax.rem(y - z_low + n_y, n_y)
    relayed_dev = dev(z, relayed_y, 1 - c, x)
    final_dev = dev((1 - c) * n_y + relayed_y, y, lax.div(z, n_y), x)
    from_core = lax.div(z, n_y)
    from_y = lax.rem(z, n_y)
    y_node = lax.rem(y - from_y + n_y, n_y)
    source_dev = dev(c * n_y + y_node, y, 1 - from_core, x)
    z_node = from_y * 2 + from_core

    def x_peer(k):
        return dev(z, y, c, lax.rem(x + k, n_x))

    def group_peer(k):
        return dev(z, y, lax.rem(c + k // n_x, 2), lax.rem(x + k % n_x, n_x))

    def y_peer(k):
        return dev(z, lax.rem(y + k, n_y), c, x)

    def z_peer(k):
        return dev(lax.rem(z + k, n_z), y, c, x)

    fetch_in = pltpu.make_async_copy(w_in_hbm, s.w_in, s.local.at[0])
    fetch_out = pltpu.make_async_copy(w_out_hbm, s.w_out, s.local.at[1])
    fetch_in.start()
    fetch_out.start()

    barrier = pltpu.get_barrier_semaphore()
    everyone = [relay_dev, relayed_dev, final_dev, source_dev]
    everyone += [group_peer(k) for k in range(1, 2 * n_x)]
    everyone += [y_peer(k) for k in range(1, n_y)]
    everyone += [z_peer(k) for k in range(1, n_z)]
    for peer in everyone:
        pl.semaphore_signal(barrier, inc=1, device_id=peer, device_id_type=MESH)
    pl.semaphore_wait(barrier, len(everyone))

    sent = []

    def push(src, dst, send_sem, recv_sem, peer):
        copy = pltpu.make_async_remote_copy(
            src_ref=src,
            dst_ref=dst,
            send_sem=send_sem,
            recv_sem=recv_sem,
            device_id=peer,
            device_id_type=MESH,
        )
        copy.start()
        sent.append(copy)
        return copy

    pieces = pieces_of(quarter)
    share = block(x * quarter, quarter, 16)
    x_from, target_from = x_hbm.at[share], target_hbm.at[share]
    hops = []
    for p, (start, size) in enumerate(pieces):
        at = pl.ds(start, size)
        hops.append(
            push(x_from.at[at], s.relay.at[at], s.hop1_s.at[p], s.hop1_r.at[p], relay_dev)
        )
    order_rows = tile_of(width)

    @pl.loop(0, width // order_rows)
    def _(step):
        base = step * order_rows
        i = lax.broadcasted_iota(jnp.int32, (order_rows, 128), 0) + base
        core_part = (i >= half).astype(jnp.int32)
        i = i - core_part * half
        y_part = jnp.zeros_like(i)
        for k in range(1, n_y):
            y_part = y_part + (i >= k * part).astype(jnp.int32)
        i = i - y_part * part
        z_part = jnp.zeros_like(i)
        for k in range(1, n_z):
            z_part = z_part + (i >= k * own).astype(jnp.int32)
        i = i - z_part * own
        column = ((z_part * n_y + y_part) * 2 + core_part) * own + i
        lanes = lax.broadcasted_iota(jnp.int32, (order_rows, 128), 1)
        for j in range(0, width, 128):
            size = min(128, width - j)
            hot = jnp.where(column == lanes + j, 1.0, 0.0)
            s.order[block(base, order_rows, 16), j : j + size] = hot[:, :size].astype(BF16)

    moved = []
    for p, (start, size) in enumerate(pieces):
        hops[p].wait_recv()
        moved.append(
            push(
                s.relay.at[pl.ds(start, size)],
                s.x.at[block(x * quarter + start, size, 16)],
                s.hop2_s.at[p],
                s.hop2_r.at[p],
                final_dev,
            )
        )
    last_piece = len(pieces)
    hops.append(
        push(
            target_from,
            s.target_relay,
            s.hop1_s.at[last_piece],
            s.hop1_r.at[last_piece],
            relay_dev,
        )
    )

    fetch_out.wait()

    def reorder_w(t):
        cols = pl.ds(t * width_tile, width_tile)
        s.w_back[:, cols] = lax.dot_general(
            s.w_out[...], s.order[cols, :], BY_ROWS, preferred_element_type=F32
        ).astype(BF16)

    near = sorted({1, n_x - 1})
    relays = [(p, near[p * len(near) // len(pieces)]) for p in (0, 2, 1, 3)]

    def rows_of(k, p):
        start, size = pieces[p]
        return block(lax.rem(x - k + n_x, n_x) * quarter + start, size, 16)

    def give(ref, p, send_sem, recv_sem):
        at = rows_of(0, p)
        return {
            (k, p): push(ref.at[at], ref.at[at], send_sem.at[p, k], recv_sem.at[p, k], x_peer(k))
            for k in near
        }

    def relay(ref, given, send_sem, recv_sem):
        if n_x == 4:
            for p, k in relays:
                given[(k, p)].wait_recv()
                at = rows_of(k, p)
                given[(2, p)] = push(
                    ref.at[at], ref.at[at], send_sem.at[p, 2], recv_sem.at[p, 2], x_peer(k)
                )

    def take(given, k):
        for p in range(len(pieces)):
            if n_x < 4 or (p, k) not in relays:
                given[(k, p)].wait_recv()

    given = {}
    for p in range(len(pieces)):
        moved[p].wait_recv()
        given.update(give(s.x, p, s.x_s, s.x_r))
        if p < width // width_tile:
            reorder_w(p)
    for t in range(len(pieces), width // width_tile):
        reorder_w(t)

    fetch_in.wait()

    steps = [0] + sorted(range(1, n_x), key=lambda k: min(k, n_x - k))
    partials = []
    for k in steps:
        r = lax.rem(x - k + n_x, n_x)
        at = block(r * quarter, quarter, 16)
        if k == 1:
            relay(s.x, given, s.x_s, s.x_r)
            hops[last_piece].wait_recv()
            moved.append(
                push(
                    s.target_relay,
                    s.target,
                    s.hop2_s.at[last_piece],
                    s.hop2_r.at[last_piece],
                    final_dev,
                )
            )
        if k:
            take(given, k)

        @pl.loop(0, hidden // hidden_tile)
        def _(j):
            cols = block(j * hidden_tile, hidden_tile, hidden_tile)
            v = jnp.dot(s.x[at, :], s.w_in[:, cols], preferred_element_type=F32)
            v2 = v * v
            t = jnp.tanh(GELU_A * (v + GELU_B * (v * v2)))
            s.hid[at, cols] = (0.5 * v * (1.0 + t)).astype(BF16)
            s.slope[at, cols] = 0.5 * (1.0 + t) + (0.5 * v) * (1.0 - t * t) * (
                GELU_A * (1.0 + (3.0 * GELU_B) * v2)
            )

        for t in range(width // width_tile):
            cols = pl.ds(t * width_tile, width_tile)
            o = jnp.dot(s.hid[at, :], s.w_back[:, cols], preferred_element_type=F32)
            if k == 0:
                s.out_own[:, cols] = o
            else:
                s.out_send[k - 1, t] = o.astype(BF16)
                partials.append(
                    push(
                        s.out_send.at[k - 1, t],
                        s.out_recv.at[k - 1, t],
                        s.out_s.at[t, k],
                        s.out_r.at[t, k],
                        dev(z, y, c, r),
                    )
                )

    @pl.loop(0, width // order_rows)
    def _(step):
        at = block(step * order_rows, order_rows, 16)
        s.x_t[at, :] = lax.dot_general(
            s.order[at, :], s.x[...], BY_ROWS, preferred_element_type=F32
        ).astype(BF16)

    moved[last_piece].wait_recv()

    @pl.loop(0, width // width_tile)
    def _(j):
        cols = block(j * width_tile, width_tile, width_tile)
        s.target_back[:, cols] = lax.dot_general(
            s.target[...], s.order[cols, :], BY_ROWS, preferred_element_type=F32
        ).astype(BF16)

    for copy in partials:
        copy.wait_recv()

    @pl.loop(0, quarter // 16)
    def _(i):
        at = block(i * 16, 16, 16)
        for t in range(width // width_tile):
            cols = pl.ds(t * width_tile, width_tile)
            total = s.out_own[at, cols]
            for k in range(1, n_x):
                total = total + s.out_recv[k - 1, t, at, :].astype(F32)
            error = (total - s.target_back[at, cols].astype(F32)) / rows
            s.err[block(x * quarter + i * 16, 16, 16), cols] = error.astype(BF16)

    given = {}
    for p in range(len(pieces)):
        given.update(give(s.err, p, s.err_s, s.err_r))
    mine = block(c * half, half, 16)
    theirs = block((1 - c) * half, half, 16)
    partner = dev(z, y, 1 - c, x)
    crossed = []

    def cross(m):
        crossed.append(push(s.send.at[m], s.recv.at[m], s.core_s.at[m], s.core_r.at[m], partner))

    def gradient_first(at, store):
        @pl.loop(0, hidden // hidden_tile)
        def _(j):
            cols = block(j * hidden_tile, hidden_tile, hidden_tile)
            store(cols, jnp.dot(s.x_t[at, :], s.dpre[:, cols], preferred_element_type=F32))

    def store_send(cols, value):
        s.send[0, :, cols] = value.astype(BF16)

    def store_keep(cols, value):
        s.keep[:, cols] = value

    for turn, k in enumerate(steps):
        r = lax.rem(x - k + n_x, n_x)
        at = block(r * quarter, quarter, 16)
        if k == 1:
            relay(s.err, given, s.err_s, s.err_r)
        if k:
            take(given, k)

        @pl.loop(0, hidden // hidden_tile)
        def _(j):
            cols = block(j * hidden_tile, hidden_tile, hidden_tile)
            back = lax.dot_general(
                s.err[at, :], s.w_back[cols, :], BY_ROWS, preferred_element_type=F32
            )
            s.dpre[at, cols] = (back * s.slope[at, cols]).astype(BF16)

        last = turn == len(steps) - 1
        if last:
            gradient_first(theirs, store_send)
            cross(0)

        for t in range(width // width_tile):
            cols = pl.ds(t * width_tile, width_tile)
            s.err_t[k, cols, :] = s.err[at, cols].T

        @pl.loop(0, hidden // hidden_tile)
        def _(j):
            cols = block(j * hidden_tile, hidden_tile, hidden_tile)
            if last:
                s.send[1, :, cols] = (
                    s.second[theirs, cols]
                    + jnp.dot(s.err_t[k, theirs, :], s.hid[at, cols], preferred_element_type=F32)
                ).astype(BF16)
                s.second[mine, cols] += jnp.dot(
                    s.err_t[k, mine, :], s.hid[at, cols], preferred_element_type=F32
                )
            else:
                value = jnp.dot(s.err_t[k], s.hid[at, cols], preferred_element_type=F32)
                if turn == 0:
                    s.second[:, cols] = value
                else:
                    s.second[:, cols] += value

        if last:
            cross(1)
            gradient_first(mine, store_keep)

    def own_part(m, start):
        if m == 0:
            return s.keep[block(start, 16, 16), :]
        return s.second[block(c * half + start, 16, 16), :]

    def total_over(buffer, send_sem, recv_sem, peer_of, count):
        copies = [
            push(buffer.at[0], buffer.at[k], send_sem.at[k], recv_sem.at[k], peer_of(k))
            for k in range(1, count)
        ]
        for copy in copies:
            copy.wait_recv()
        total = buffer[0]
        for k in range(1, count):
            total = total + buffer[k]
        return total

    stats = (jnp.zeros((8, 128), F32),) * 3
    for m in range(2):
        crossed[m].wait_recv()

        def level_sums(i, carry):
            at = block(i * 16, 16, 16)
            a = own_part(m, i * 16)
            b = s.recv[m, at, :].astype(F32)
            return (carry[0] + fold(a * b), carry[1] + fold(a * a), carry[2] + fold(b * b))

        stats = lax.fori_loop(0, half // 16, level_sums, stats)
    is_low = c == 0
    s.a0[0] = pack(
        s.r0,
        (
            stats[0],
            jnp.where(is_low, stats[1], stats[2]),
            jnp.where(is_low, stats[2], stats[1]),
        ),
    )
    total = total_over(s.a0, s.a0_s, s.a0_r, group_peer, 2 * n_x)
    weights = tree_weights(unpack(total, ((0, 1), (0, 0), (1, 1)), 8), 2)
    weight_own = jnp.where(is_low, weights[0], weights[1])
    weight_other = jnp.where(is_low, weights[1], weights[0])

    y_copies = [[], []]
    for m in range(2):
        for k in list(range(1, n_y)) + [0]:
            part_at = lax.rem(y + k, n_y) * part

            @pl.loop(0, part // 16)
            def _(i):
                at = block(part_at + i * 16, 16, 16)
                node = weight_own * own_part(m, part_at + i * 16)
                node = (node + weight_other * s.recv[m, at, :].astype(F32)).astype(BF16)
                if k:
                    s.node[m, at, :] = node
                else:
                    s.y_recv[y_node, m, block(i * 16, 16, 16), :] = node

            if k:
                y_copies[m].append(
                    push(
                        s.node.at[m, block(part_at, part, 16)],
                        s.y_recv.at[y_node, m],
                        s.y_s.at[m, k],
                        s.y_r.at[m, k],
                        y_peer(k),
                    )
                )

    y_pairs = pairs_of(n_y)

    stats = (jnp.zeros((8, 128), F32),) * len(y_pairs)
    for m in range(2):
        for copy in y_copies[m]:
            copy.wait_recv()

        def y_sums(i, carry):
            at = block(i * 16, 16, 16)
            nodes = [s.y_recv[j, m, at, :].astype(F32) for j in range(n_y)]
            return tuple(old + fold(nodes[a] * nodes[b]) for old, (a, b) in zip(carry, y_pairs))

        stats = lax.fori_loop(0, part // 16, y_sums, stats)
    s.a1[0] = pack(s.r1, stats)
    s.b1[0] = total_over(s.a1, s.a1_s, s.a1_r, group_peer, 2 * n_x)
    total = total_over(s.b1, s.b1_s, s.b1_r, y_peer, n_y)
    weights = tree_weights(unpack(total, y_pairs, s.r1.shape[0]), n_y)

    @pl.loop(0, part // 16)
    def _(i):
        at = block(i * 16, 16, 16)
        for m in range(2):
            merged = weights[0] * s.y_recv[0, m, at, :].astype(F32)
            for j in range(1, n_y):
                merged = merged + weights[j] * s.y_recv[j, m, at, :].astype(F32)
            s.y_merged[m, at, :] = merged

    for j in range(n_z):
        for m in range(2):
            s.z_send[j, m] = s.y_merged[m, j * own : (j + 1) * own, :].astype(BF16)

    z_copies = []
    for k in range(1, n_z):
        z_copies.append(
            push(
                s.z_send.at[lax.rem(z + k, n_z)],
                s.z_recv.at[z_node],
                s.z_s.at[k],
                s.z_r.at[k],
                z_peer(k),
            )
        )
    s.z_recv[z_node] = s.z_send[z]
    for copy in z_copies:
        copy.wait_recv()

    z_pairs = pairs_of(n_z)
    stats = []
    for a, b in z_pairs:
        value = 0.0
        for m in range(2):
            value = value + s.z_recv[a, m].astype(F32) * s.z_recv[b, m].astype(F32)
        stats.append(fold_row(value))
    s.a2[0] = pack(s.r2, stats)
    s.b2[0] = total_over(s.a2, s.a2_s, s.a2_r, group_peer, 2 * n_x)
    s.c2[0] = total_over(s.b2, s.b2_s, s.b2_r, y_peer, n_y)
    total = total_over(s.c2, s.c2_s, s.c2_r, z_peer, n_z)
    weights = tree_weights(unpack(total, z_pairs, s.r2.shape[0]), n_z)
    for m, out in enumerate((first_out, second_out)):
        merged = weights[0] * s.z_recv[0, m].astype(F32)
        for j in range(1, n_z):
            merged = merged + weights[j] * s.z_recv[j, m].astype(F32)
        out[...] = merged
    for copy in sent:
        copy.wait_send()


def solution(mesh):
    n_x = mesh.shape["tensor"]
    n_y = math.isqrt(mesh.shape["dp"] // 4)

    def on_device(inputs, targets, w_in, w_out):
        rows, width = inputs.shape
        hidden = w_in.shape[1]
        scratch = scratch_of(n_x, n_y, rows, width, hidden)
        share = jax.ShapeDtypeStruct((width // mesh.shape["dp"], hidden), F32)
        return pl.pallas_call(
            functools.partial(kernel, n_x, n_y, tuple(scratch)),
            out_shape=(share, share),
            in_specs=[pl.BlockSpec(memory_space=pl.ANY)] * 4,
            out_specs=(pl.BlockSpec(memory_space=pltpu.VMEM),) * 2,
            scratch_shapes=list(scratch.values()),
            compiler_params=pltpu.CompilerParams(
                collective_id=0, has_side_effects=True, vmem_limit_bytes=67_000_000
            ),
        )(inputs, targets, w_in, w_out)

    placed = (P("dp", None), P("dp", None), P(None, "tensor"), P("tensor", None))
    return jax.shard_map(
        on_device,
        mesh=mesh,
        in_specs=placed,
        out_specs=(P("dp", "tensor"), P("dp", "tensor")),
        check_vma=False,
    )
```

```python
import functools
import math

import jax
import jax.numpy as jnp
from jax import lax
from jax.experimental import pallas as pl
from jax.experimental.pallas import tpu as pltpu
from jax.sharding import PartitionSpec as P

F32, BF16 = jnp.float32, jnp.bfloat16
EPSILON = 1e-06
GELU_A = math.sqrt(2.0 / math.pi)
GELU_B = 0.044715
MESH = pl.DeviceIdType.MESH
BY_ROWS = (((1,), (1,)), ((), ()))


def tile_of(n):
    return 256 if n % 256 == 0 else n


def block(start, size, step):
    return pl.ds(pl.multiple_of(start, step), size)


def fold(v):
    rows, columns = v.shape
    t = v[0:8]
    for i in range(8, rows, 8):
        t = t + v[i : i + 8]
    s = t[:, :128]
    for j in range(128, columns, 128):
        s = s + t[:, j : j + 128]
    return s


def fold_row(v):
    t = jnp.sum(v, axis=0, keepdims=True)
    s = t[:, :128]
    for j in range(128, v.shape[1], 128):
        s = s + t[:, j : j + 128]
    return s


def pieces_of(rows):
    units, pieces = rows // 16, []
    for p in range(4):
        start = p * units // 4
        pieces.append((start * 16, ((p + 1) * units // 4 - start) * 16))
    return pieces


def groups_of(n_x):
    return [[0], [1, 3], [2]] if n_x == 4 else [[k] for k in range(n_x)]


def diagonal(n):
    shape = (n, 128)
    return lax.broadcasted_iota(jnp.int32, shape, 0) == lax.broadcasted_iota(jnp.int32, shape, 1)


def pack(rows, values):
    rows[...] = jnp.zeros(rows.shape, F32)
    for i, value in enumerate(values):
        rows[i : i + 1, :] = jnp.sum(value, axis=0, keepdims=True)
    column = jnp.sum(rows[...], axis=1, keepdims=True)
    line = jnp.sum(jnp.where(diagonal(rows.shape[0]), column, 0.0), axis=0, keepdims=True)
    return jnp.broadcast_to(line, (8, 128))


def unpack(total, names, n):
    line = jnp.broadcast_to(total[0:1], (n, 128))
    column = jnp.sum(jnp.where(diagonal(n), line, 0.0), axis=1, keepdims=True)
    return {name: column[i : i + 1] for i, name in enumerate(names)}


def pairs_of(n):
    return [(i, j) for i in range(n) for j in range(i, n)]


def tree_weights(gram, n):
    if n == 1:
        return [None]
    half = n // 2

    def at(i, j):
        return gram[(min(i, j), max(i, j))]

    low, high = [], []
    for j in range(half):
        product = at(j, j + half)
        low.append(1.0 - product / (2.0 * (at(j, j) + EPSILON)))
        high.append(1.0 - product / (2.0 * (at(j + half, j + half) + EPSILON)))
    if half == 1:
        return low + high
    merged = {}
    for j, k in pairs_of(half):
        merged[(j, k)] = (
            low[j] * low[k] * at(j, k)
            + low[j] * high[k] * at(j, k + half)
            + high[j] * low[k] * at(j + half, k)
            + high[j] * high[k] * at(j + half, k + half)
        )
    outer = tree_weights(merged, half)
    return [outer[j] * low[j] for j in range(half)] + [outer[j] * high[j] for j in range(half)]


def scratch_of(n_x, n_y, rows, width, hidden):
    n_z = 2 * n_y
    quarter = rows // n_x
    half, part, own = width // 2, width // (2 * n_y), width // (2 * n_y * n_z)
    stat_y = -(-len(pairs_of(n_y)) // 8) * 8
    stat_z = -(-len(pairs_of(n_z)) // 8) * 8
    everyone = 2 * n_x
    tiles = width // tile_of(width)
    dma = pltpu.SemaphoreType.DMA
    return {
        "w_in": pltpu.VMEM((width, hidden), BF16),
        "w_out": pltpu.VMEM((hidden, width), BF16),
        "w_back": pltpu.VMEM((hidden, width), BF16),
        "target_back": pltpu.VMEM((quarter, width), BF16),
        "x": pltpu.VMEM((rows, width), BF16),
        "target": pltpu.VMEM((quarter, width), BF16),
        "order": pltpu.VMEM((width, width), BF16),
        "x_t": pltpu.VMEM((width, rows), BF16),
        **{
            f"err_t{i}": pltpu.VMEM((width, len(group) * quarter), BF16)
            for i, group in enumerate(groups_of(n_x))
        },
        "hid": pltpu.VMEM((rows, hidden), BF16),
        "slope": pltpu.VMEM((rows, hidden), F32),
        "out_own": pltpu.VMEM((quarter, width), F32),
        "out_send": pltpu.VMEM((n_x - 1, tiles, quarter, width // tiles), BF16),
        "out_recv": pltpu.VMEM((n_x - 1, tiles, quarter, width // tiles), BF16),
        "err": pltpu.VMEM((rows, width), BF16),
        "dpre": pltpu.VMEM((rows, hidden), BF16),
        "keep": pltpu.VMEM((half, hidden), F32),
        "second": pltpu.VMEM((width, hidden), F32),
        "send": pltpu.VMEM((2, half, hidden), BF16),
        "recv": pltpu.VMEM((2, half, hidden), BF16),
        "node": pltpu.VMEM((2, half, hidden), BF16),
        "y_recv": pltpu.VMEM((n_y, 2, part, hidden), BF16),
        "y_merged": pltpu.VMEM((2, part, hidden), F32),
        "z_send": pltpu.VMEM((n_z, 2, own, hidden), BF16),
        "z_recv": pltpu.VMEM((n_z, 2, own, hidden), BF16),
        "r0": pltpu.VMEM((8, 128), F32),
        "r1": pltpu.VMEM((stat_y, 128), F32),
        "r2": pltpu.VMEM((stat_z, 128), F32),
        "a0": pltpu.VMEM((everyone, 8, 128), F32),
        "a1": pltpu.VMEM((everyone, 8, 128), F32),
        "b1": pltpu.VMEM((n_y, 8, 128), F32),
        "a2": pltpu.VMEM((everyone, 8, 128), F32),
        "b2": pltpu.VMEM((n_y, 8, 128), F32),
        "c2": pltpu.VMEM((n_z, 8, 128), F32),
        "local": dma((2,)),
        "relay": pltpu.VMEM((quarter, width), BF16),
        "target_relay": pltpu.VMEM((quarter, width), BF16),
        "hop1_s": dma((5,)),
        "hop1_r": dma((5,)),
        "hop2_s": dma((5,)),
        "hop2_r": dma((5,)),
        "x_s": dma((4, n_x)),
        "x_r": dma((4, n_x)),
        "out_s": dma((tiles, n_x)),
        "out_r": dma((tiles, n_x)),
        "err_s": dma((4, n_x)),
        "err_r": dma((4, n_x)),
        "core_s": dma((2,)),
        "core_r": dma((2,)),
        "y_s": dma((2, n_y)),
        "y_r": dma((2, n_y)),
        "z_s": dma((n_z,)),
        "z_r": dma((n_z,)),
        "a0_s": dma((everyone,)),
        "a0_r": dma((everyone,)),
        "a1_s": dma((everyone,)),
        "a1_r": dma((everyone,)),
        "b1_s": dma((n_y,)),
        "b1_r": dma((n_y,)),
        "a2_s": dma((everyone,)),
        "a2_r": dma((everyone,)),
        "b2_s": dma((n_y,)),
        "b2_r": dma((n_y,)),
        "c2_s": dma((n_z,)),
        "c2_r": dma((n_z,)),
    }


class Refs:
    pass


def kernel(n_x, n_y, names, x_hbm, target_hbm, w_in_hbm, w_out_hbm, first_out, second_out, *scratch):
    s = Refs()
    for name, ref in zip(names, scratch):
        setattr(s, name, ref)
    n_z = 2 * n_y
    rows, width = x_hbm.shape
    hidden = w_in_hbm.shape[1]
    quarter = rows // n_x
    half, part, own = width // 2, width // (2 * n_y), width // (2 * n_y * n_z)
    width_tile, hidden_tile = tile_of(width), tile_of(hidden)

    me = lax.axis_index("dp")
    x = lax.axis_index("tensor")
    c = lax.rem(me, 2)
    y = lax.rem(lax.div(me, 2), n_y)
    z = lax.div(me, 2 * n_y)

    def dev(z_, y_, c_, x_):
        return {"dp": (z_ * n_y + y_) * 2 + c_, "tensor": x_}

    z_low = lax.rem(z, n_y)
    relay_dev = dev(z, lax.rem(y + z_low, n_y), 1 - c, x)
    relayed_y = lax.rem(y - z_low + n_y, n_y)
    relayed_dev = dev(z, relayed_y, 1 - c, x)
    final_dev = dev((1 - c) * n_y + relayed_y, y, lax.div(z, n_y), x)
    from_core = lax.div(z, n_y)
    from_y = lax.rem(z, n_y)
    y_node = lax.rem(y - from_y + n_y, n_y)
    source_dev = dev(c * n_y + y_node, y, 1 - from_core, x)
    z_node = from_y * 2 + from_core

    def x_peer(k):
        return dev(z, y, c, lax.rem(x + k, n_x))

    def group_peer(k):
        return dev(z, y, lax.rem(c + k // n_x, 2), lax.rem(x + k % n_x, n_x))

    def y_peer(k):
        return dev(z, lax.rem(y + k, n_y), c, x)

    def z_peer(k):
        return dev(lax.rem(z + k, n_z), y, c, x)

    fetch_in = pltpu.make_async_copy(w_in_hbm, s.w_in, s.local.at[0])
    fetch_out = pltpu.make_async_copy(w_out_hbm, s.w_out, s.local.at[1])
    fetch_in.start()
    fetch_out.start()

    barrier = pltpu.get_barrier_semaphore()
    everyone = [relay_dev, relayed_dev, final_dev, source_dev]
    everyone += [group_peer(k) for k in range(1, 2 * n_x)]
    everyone += [y_peer(k) for k in range(1, n_y)]
    everyone += [z_peer(k) for k in range(1, n_z)]
    for peer in everyone:
        pl.semaphore_signal(barrier, inc=1, device_id=peer, device_id_type=MESH)
    pl.semaphore_wait(barrier, len(everyone))

    sent = []

    def push(src, dst, send_sem, recv_sem, peer):
        copy = pltpu.make_async_remote_copy(
            src_ref=src,
            dst_ref=dst,
            send_sem=send_sem,
            recv_sem=recv_sem,
            device_id=peer,
            device_id_type=MESH,
        )
        copy.start()
        sent.append(copy)
        return copy

    pieces = pieces_of(quarter)
    share = block(x * quarter, quarter, 16)
    x_from, target_from = x_hbm.at[share], target_hbm.at[share]
    hops = []
    for p, (start, size) in enumerate(pieces):
        at = pl.ds(start, size)
        hops.append(
            push(x_from.at[at], s.relay.at[at], s.hop1_s.at[p], s.hop1_r.at[p], relay_dev)
        )
    order_rows = tile_of(width)

    @pl.loop(0, width // order_rows)
    def _(step):
        base = step * order_rows
        i = lax.broadcasted_iota(jnp.int32, (order_rows, 128), 0) + base
        core_part = (i >= half).astype(jnp.int32)
        i = i - core_part * half
        y_part = jnp.zeros_like(i)
        for k in range(1, n_y):
            y_part = y_part + (i >= k * part).astype(jnp.int32)
        i = i - y_part * part
        z_part = jnp.zeros_like(i)
        for k in range(1, n_z):
            z_part = z_part + (i >= k * own).astype(jnp.int32)
        i = i - z_part * own
        column = ((z_part * n_y + y_part) * 2 + core_part) * own + i
        lanes = lax.broadcasted_iota(jnp.int32, (order_rows, 128), 1)
        for j in range(0, width, 128):
            size = min(128, width - j)
            hot = jnp.where(column == lanes + j, 1.0, 0.0)
            s.order[block(base, order_rows, 16), j : j + size] = hot[:, :size].astype(BF16)

    moved = []
    for p, (start, size) in enumerate(pieces):
        hops[p].wait_recv()
        moved.append(
            push(
                s.relay.at[pl.ds(start, size)],
                s.x.at[pl.ds(start, size)],
                s.hop2_s.at[p],
                s.hop2_r.at[p],
                final_dev,
            )
        )
    last_piece = len(pieces)
    hops.append(
        push(
            target_from,
            s.target_relay,
            s.hop1_s.at[last_piece],
            s.hop1_r.at[last_piece],
            relay_dev,
        )
    )

    fetch_out.wait()

    def reorder_w(t):
        cols = pl.ds(t * width_tile, width_tile)
        s.w_back[:, cols] = lax.dot_general(
            s.w_out[...], s.order[cols, :], BY_ROWS, preferred_element_type=F32
        ).astype(BF16)

    near = sorted({1, n_x - 1})
    groups = groups_of(n_x)
    slot = {k: i for i, k in enumerate(k for group in groups for k in group)}
    relays = [(p, near[p * len(near) // len(pieces)]) for p in (0, 2, 1, 3)]

    def rows_of(k, p):
        start, size = pieces[p]
        return pl.ds(slot[k] * quarter + start, size)

    def give(ref, p, send_sem, recv_sem):
        at = rows_of(0, p)
        return {
            (k, p): push(
                ref.at[at], ref.at[rows_of(k, p)], send_sem.at[p, k], recv_sem.at[p, k], x_peer(k)
            )
            for k in near
        }

    def relay(ref, given, send_sem, recv_sem):
        if n_x == 4:
            for p, k in relays:
                given[(k, p)].wait_recv()
                at = rows_of(k, p)
                given[(2, p)] = push(
                    ref.at[at],
                    ref.at[rows_of(2, p)],
                    send_sem.at[p, 2],
                    recv_sem.at[p, 2],
                    x_peer(k),
                )

    def take(given, k):
        for p in range(len(pieces)):
            if n_x < 4 or (p, k) not in relays:
                given[(k, p)].wait_recv()

    given = {}
    for p in range(len(pieces)):
        moved[p].wait_recv()
        given.update(give(s.x, p, s.x_s, s.x_r))
        if p < width // width_tile:
            reorder_w(p)
    for t in range(len(pieces), width // width_tile):
        reorder_w(t)

    fetch_in.wait()

    partials = []
    for turn, group in enumerate(groups):
        at = pl.ds(slot[group[0]] * quarter, len(group) * quarter)
        if turn == 1:
            relay(s.x, given, s.x_s, s.x_r)
            hops[last_piece].wait_recv()
            moved.append(
                push(
                    s.target_relay,
                    s.target,
                    s.hop2_s.at[last_piece],
                    s.hop2_r.at[last_piece],
                    final_dev,
                )
            )
        for k in group:
            if k:
                take(given, k)

        @pl.loop(0, hidden // hidden_tile)
        def _(j):
            cols = block(j * hidden_tile, hidden_tile, hidden_tile)
            v = jnp.dot(s.x[at, :], s.w_in[:, cols], preferred_element_type=F32)
            v2 = v * v
            t = jnp.tanh(GELU_A * (v + GELU_B * (v * v2)))
            s.hid[at, cols] = (0.5 * v * (1.0 + t)).astype(BF16)
            s.slope[at, cols] = 0.5 * (1.0 + t) + (0.5 * v) * (1.0 - t * t) * (
                GELU_A * (1.0 + (3.0 * GELU_B) * v2)
            )

        for t in range(width // width_tile):
            cols = pl.ds(t * width_tile, width_tile)
            o = jnp.dot(s.hid[at, :], s.w_back[:, cols], preferred_element_type=F32)
            for i, k in enumerate(group):
                if k == 0:
                    s.out_own[:, cols] = o
                    continue
                s.out_send[k - 1, t] = o[i * quarter : (i + 1) * quarter].astype(BF16)
                partials.append(
                    push(
                        s.out_send.at[k - 1, t],
                        s.out_recv.at[k - 1, t],
                        s.out_s.at[t, k],
                        s.out_r.at[t, k],
                        x_peer(n_x - k),
                    )
                )

    @pl.loop(0, width // order_rows)
    def _(step):
        at = block(step * order_rows, order_rows, 16)
        s.x_t[at, :] = lax.dot_general(
            s.order[at, :], s.x[...], BY_ROWS, preferred_element_type=F32
        ).astype(BF16)

    moved[last_piece].wait_recv()

    @pl.loop(0, width // width_tile)
    def _(j):
        cols = block(j * width_tile, width_tile, width_tile)
        s.target_back[:, cols] = lax.dot_general(
            s.target[...], s.order[cols, :], BY_ROWS, preferred_element_type=F32
        ).astype(BF16)

    for copy in partials:
        copy.wait_recv()

    @pl.loop(0, quarter // 16)
    def _(i):
        at = block(i * 16, 16, 16)
        for t in range(width // width_tile):
            cols = pl.ds(t * width_tile, width_tile)
            total = s.out_own[at, cols]
            for k in range(1, n_x):
                total = total + s.out_recv[k - 1, t, at, :].astype(F32)
            error = (total - s.target_back[at, cols].astype(F32)) / rows
            s.err[at, cols] = error.astype(BF16)

    given = {}
    for p in range(len(pieces)):
        given.update(give(s.err, p, s.err_s, s.err_r))
    mine = block(c * half, half, 16)
    theirs = block((1 - c) * half, half, 16)
    partner = dev(z, y, 1 - c, x)
    crossed = []

    def cross(m):
        crossed.append(push(s.send.at[m], s.recv.at[m], s.core_s.at[m], s.core_r.at[m], partner))

    def gradient_first(at, store):
        @pl.loop(0, hidden // hidden_tile)
        def _(j):
            cols = block(j * hidden_tile, hidden_tile, hidden_tile)
            store(cols, jnp.dot(s.x_t[at, :], s.dpre[:, cols], preferred_element_type=F32))

    def store_send(cols, value):
        s.send[0, :, cols] = value.astype(BF16)

    def store_keep(cols, value):
        s.keep[:, cols] = value

    for turn, group in enumerate(groups):
        at = pl.ds(slot[group[0]] * quarter, len(group) * quarter)
        err_t = getattr(s, f"err_t{turn}")
        if turn == 1:
            relay(s.err, given, s.err_s, s.err_r)
        for k in group:
            if k:
                take(given, k)

        @pl.loop(0, hidden // hidden_tile)
        def _(j):
            cols = block(j * hidden_tile, hidden_tile, hidden_tile)
            back = lax.dot_general(
                s.err[at, :], s.w_back[cols, :], BY_ROWS, preferred_element_type=F32
            )
            s.dpre[at, cols] = (back * s.slope[at, cols]).astype(BF16)

        last = turn == len(groups) - 1
        if last:
            gradient_first(theirs, store_send)
            cross(0)

        for t in range(width // width_tile):
            cols = pl.ds(t * width_tile, width_tile)
            err_t[cols, :] = s.err[at, cols].T

        @pl.loop(0, hidden // hidden_tile)
        def _(j):
            cols = block(j * hidden_tile, hidden_tile, hidden_tile)
            if last:
                s.send[1, :, cols] = (
                    s.second[theirs, cols]
                    + jnp.dot(err_t[theirs, :], s.hid[at, cols], preferred_element_type=F32)
                ).astype(BF16)
                s.second[mine, cols] += jnp.dot(
                    err_t[mine, :], s.hid[at, cols], preferred_element_type=F32
                )
            else:
                value = jnp.dot(err_t[...], s.hid[at, cols], preferred_element_type=F32)
                if turn == 0:
                    s.second[:, cols] = value
                else:
                    s.second[:, cols] += value

        if last:
            cross(1)
            gradient_first(mine, store_keep)

    def own_part(m, start):
        if m == 0:
            return s.keep[block(start, 16, 16), :]
        return s.second[block(c * half + start, 16, 16), :]

    def total_over(buffer, send_sem, recv_sem, peer_of, count):
        copies = [
            push(buffer.at[0], buffer.at[k], send_sem.at[k], recv_sem.at[k], peer_of(k))
            for k in range(1, count)
        ]
        for copy in copies:
            copy.wait_recv()
        total = buffer[0]
        for k in range(1, count):
            total = total + buffer[k]
        return total

    stats = (jnp.zeros((8, 128), F32),) * 3
    for m in range(2):
        crossed[m].wait_recv()

        def level_sums(i, carry):
            at = block(i * 16, 16, 16)
            a = own_part(m, i * 16)
            b = s.recv[m, at, :].astype(F32)
            return (carry[0] + fold(a * b), carry[1] + fold(a * a), carry[2] + fold(b * b))

        stats = lax.fori_loop(0, half // 16, level_sums, stats)
    is_low = c == 0
    s.a0[0] = pack(
        s.r0,
        (
            stats[0],
            jnp.where(is_low, stats[1], stats[2]),
            jnp.where(is_low, stats[2], stats[1]),
        ),
    )
    total = total_over(s.a0, s.a0_s, s.a0_r, group_peer, 2 * n_x)
    weights = tree_weights(unpack(total, ((0, 1), (0, 0), (1, 1)), 8), 2)
    weight_own = jnp.where(is_low, weights[0], weights[1])
    weight_other = jnp.where(is_low, weights[1], weights[0])

    y_copies = [[], []]
    for m in range(2):
        for k in list(range(1, n_y)) + [0]:
            part_at = lax.rem(y + k, n_y) * part

            @pl.loop(0, part // 16)
            def _(i):
                at = block(part_at + i * 16, 16, 16)
                node = weight_own * own_part(m, part_at + i * 16)
                node = (node + weight_other * s.recv[m, at, :].astype(F32)).astype(BF16)
                if k:
                    s.node[m, at, :] = node
                else:
                    s.y_recv[y_node, m, block(i * 16, 16, 16), :] = node

            if k:
                y_copies[m].append(
                    push(
                        s.node.at[m, block(part_at, part, 16)],
                        s.y_recv.at[y_node, m],
                        s.y_s.at[m, k],
                        s.y_r.at[m, k],
                        y_peer(k),
                    )
                )

    y_pairs = pairs_of(n_y)

    stats = (jnp.zeros((8, 128), F32),) * len(y_pairs)
    for m in range(2):
        for copy in y_copies[m]:
            copy.wait_recv()

        def y_sums(i, carry):
            at = block(i * 16, 16, 16)
            nodes = [s.y_recv[j, m, at, :].astype(F32) for j in range(n_y)]
            return tuple(old + fold(nodes[a] * nodes[b]) for old, (a, b) in zip(carry, y_pairs))

        stats = lax.fori_loop(0, part // 16, y_sums, stats)
    s.a1[0] = pack(s.r1, stats)
    s.b1[0] = total_over(s.a1, s.a1_s, s.a1_r, group_peer, 2 * n_x)
    total = total_over(s.b1, s.b1_s, s.b1_r, y_peer, n_y)
    weights = tree_weights(unpack(total, y_pairs, s.r1.shape[0]), n_y)

    @pl.loop(0, part // 16)
    def _(i):
        at = block(i * 16, 16, 16)
        for m in range(2):
            merged = weights[0] * s.y_recv[0, m, at, :].astype(F32)
            for j in range(1, n_y):
                merged = merged + weights[j] * s.y_recv[j, m, at, :].astype(F32)
            s.y_merged[m, at, :] = merged

    for j in range(n_z):
        for m in range(2):
            s.z_send[j, m] = s.y_merged[m, j * own : (j + 1) * own, :].astype(BF16)

    z_copies = []
    for k in range(1, n_z):
        z_copies.append(
            push(
                s.z_send.at[lax.rem(z + k, n_z)],
                s.z_recv.at[z_node],
                s.z_s.at[k],
                s.z_r.at[k],
                z_peer(k),
            )
        )
    s.z_recv[z_node] = s.z_send[z]
    for copy in z_copies:
        copy.wait_recv()

    z_pairs = pairs_of(n_z)
    stats = []
    for a, b in z_pairs:
        value = 0.0
        for m in range(2):
            value = value + s.z_recv[a, m].astype(F32) * s.z_recv[b, m].astype(F32)
        stats.append(fold_row(value))
    s.a2[0] = pack(s.r2, stats)
    s.b2[0] = total_over(s.a2, s.a2_s, s.a2_r, group_peer, 2 * n_x)
    s.c2[0] = total_over(s.b2, s.b2_s, s.b2_r, y_peer, n_y)
    total = total_over(s.c2, s.c2_s, s.c2_r, z_peer, n_z)
    weights = tree_weights(unpack(total, z_pairs, s.r2.shape[0]), n_z)
    for m, out in enumerate((first_out, second_out)):
        merged = weights[0] * s.z_recv[0, m].astype(F32)
        for j in range(1, n_z):
            merged = merged + weights[j] * s.z_recv[j, m].astype(F32)
        out[...] = merged
    for copy in sent:
        copy.wait_send()


def solution(mesh):
    n_x = mesh.shape["tensor"]
    n_y = math.isqrt(mesh.shape["dp"] // 4)

    def on_device(inputs, targets, w_in, w_out):
        rows, width = inputs.shape
        hidden = w_in.shape[1]
        scratch = scratch_of(n_x, n_y, rows, width, hidden)
        share = jax.ShapeDtypeStruct((width // mesh.shape["dp"], hidden), F32)
        return pl.pallas_call(
            functools.partial(kernel, n_x, n_y, tuple(scratch)),
            out_shape=(share, share),
            in_specs=[pl.BlockSpec(memory_space=pl.ANY)] * 4,
            out_specs=(pl.BlockSpec(memory_space=pltpu.VMEM),) * 2,
            scratch_shapes=list(scratch.values()),
            compiler_params=pltpu.CompilerParams(
                collective_id=0, has_side_effects=True, vmem_limit_bytes=67_000_000
            ),
        )(inputs, targets, w_in, w_out)

    placed = (P("dp", None), P("dp", None), P(None, "tensor"), P("tensor", None))
    return jax.shard_map(
        on_device,
        mesh=mesh,
        in_specs=placed,
        out_specs=(P("dp", "tensor"), P("dp", "tensor")),
        check_vma=False,
    )
```

```python
import functools
import math

import jax
import jax.numpy as jnp
from jax import lax
from jax.experimental import pallas as pl
from jax.experimental.pallas import tpu as pltpu
from jax.sharding import PartitionSpec as P

F32, BF16 = jnp.float32, jnp.bfloat16
EPSILON = 1e-06
GELU_A = math.sqrt(2.0 / math.pi)
GELU_B = 0.044715
MESH = pl.DeviceIdType.MESH
BY_ROWS = (((1,), (1,)), ((), ()))


def tile_of(n):
    return 256 if n % 256 == 0 else n


def block(start, size, step):
    return pl.ds(pl.multiple_of(start, step), size)


def fold(v):
    rows, columns = v.shape
    t = v[0:8]
    for i in range(8, rows, 8):
        t = t + v[i : i + 8]
    s = t[:, :128]
    for j in range(128, columns, 128):
        s = s + t[:, j : j + 128]
    return s


def fold_row(v):
    t = jnp.sum(v, axis=0, keepdims=True)
    s = t[:, :128]
    for j in range(128, v.shape[1], 128):
        s = s + t[:, j : j + 128]
    return s


def pieces_of(rows):
    units, pieces = rows // 16, []
    for p in range(4):
        start = p * units // 4
        pieces.append((start * 16, ((p + 1) * units // 4 - start) * 16))
    return pieces


def groups_of(n_x):
    return [[0], [1, 3], [2]] if n_x == 4 else [[k] for k in range(n_x)]


def diagonal(n):
    shape = (n, 128)
    return lax.broadcasted_iota(jnp.int32, shape, 0) == lax.broadcasted_iota(jnp.int32, shape, 1)


def pack(rows, values):
    rows[...] = jnp.zeros(rows.shape, F32)
    for i, value in enumerate(values):
        rows[i : i + 1, :] = jnp.sum(value, axis=0, keepdims=True)
    column = jnp.sum(rows[...], axis=1, keepdims=True)
    line = jnp.sum(jnp.where(diagonal(rows.shape[0]), column, 0.0), axis=0, keepdims=True)
    return jnp.broadcast_to(line, (8, 128))


def unpack(total, names, n):
    line = jnp.broadcast_to(total[0:1], (n, 128))
    column = jnp.sum(jnp.where(diagonal(n), line, 0.0), axis=1, keepdims=True)
    return {name: column[i : i + 1] for i, name in enumerate(names)}


def pairs_of(n):
    return [(i, j) for i in range(n) for j in range(i, n)]


def tree_weights(gram, n):
    if n == 1:
        return [None]
    half = n // 2

    def at(i, j):
        return gram[(min(i, j), max(i, j))]

    low, high = [], []
    for j in range(half):
        product = at(j, j + half)
        low.append(1.0 - product / (2.0 * (at(j, j) + EPSILON)))
        high.append(1.0 - product / (2.0 * (at(j + half, j + half) + EPSILON)))
    if half == 1:
        return low + high
    merged = {}
    for j, k in pairs_of(half):
        merged[(j, k)] = (
            low[j] * low[k] * at(j, k)
            + low[j] * high[k] * at(j, k + half)
            + high[j] * low[k] * at(j + half, k)
            + high[j] * high[k] * at(j + half, k + half)
        )
    outer = tree_weights(merged, half)
    return [outer[j] * low[j] for j in range(half)] + [outer[j] * high[j] for j in range(half)]


def scratch_of(n_x, n_y, rows, width, hidden):
    n_z = 2 * n_y
    quarter = rows // n_x
    half, part, own = width // 2, width // (2 * n_y), width // (2 * n_y * n_z)
    stat_y = -(-len(pairs_of(n_y)) // 8) * 8
    stat_z = -(-len(pairs_of(n_z)) // 8) * 8
    everyone, plane = 2 * n_x, 2 * n_x * n_y
    tiles = width // tile_of(width)
    dma = pltpu.SemaphoreType.DMA
    return {
        "w_in": pltpu.VMEM((width, hidden), BF16),
        "w_out": pltpu.VMEM((hidden, width), BF16),
        "w_back": pltpu.VMEM((hidden, width), BF16),
        "target_back": pltpu.VMEM((quarter, width), BF16),
        "x": pltpu.VMEM((rows, width), BF16),
        "target": pltpu.VMEM((quarter, width), BF16),
        "order": pltpu.VMEM((width, width), BF16),
        "x_t": pltpu.VMEM((width, rows), BF16),
        **{
            f"err_t{i}": pltpu.VMEM((width, len(group) * quarter), BF16)
            for i, group in enumerate(groups_of(n_x))
        },
        "hid": pltpu.VMEM((rows, hidden), BF16),
        "slope": pltpu.VMEM((rows, hidden), F32),
        "out_own": pltpu.VMEM((quarter, width), F32),
        "out_send": pltpu.VMEM((n_x - 1, tiles, quarter, width // tiles), BF16),
        "out_recv": pltpu.VMEM((n_x - 1, tiles, quarter, width // tiles), BF16),
        "err": pltpu.VMEM((rows, width), BF16),
        "dpre": pltpu.VMEM((rows, hidden), BF16),
        "keep": pltpu.VMEM((half, hidden), F32),
        "second": pltpu.VMEM((width, hidden), F32),
        "send": pltpu.VMEM((2, half, hidden), BF16),
        "recv": pltpu.VMEM((2, half, hidden), BF16),
        "node": pltpu.VMEM((2, half, hidden), BF16),
        "y_recv": pltpu.VMEM((n_y, 2, part, hidden), BF16),
        "y_merged": pltpu.VMEM((2, part, hidden), F32),
        "z_send": pltpu.VMEM((n_z, 2, own, hidden), BF16),
        "z_recv": pltpu.VMEM((n_z, 2, own, hidden), BF16),
        "r0": pltpu.VMEM((8, 128), F32),
        "r1": pltpu.VMEM((stat_y, 128), F32),
        "r2": pltpu.VMEM((stat_z, 128), F32),
        "a0": pltpu.VMEM((everyone, 8, 128), F32),
        "a1": pltpu.VMEM((plane, 8, 128), F32),
        "a2": pltpu.VMEM((plane, 8, 128), F32),
        "c2": pltpu.VMEM((n_z, 8, 128), F32),
        "local": dma((2,)),
        "relay": pltpu.VMEM((quarter, width), BF16),
        "target_relay": pltpu.VMEM((quarter, width), BF16),
        "hop1_s": dma((5,)),
        "hop1_r": dma((5,)),
        "hop2_s": dma((5,)),
        "hop2_r": dma((5,)),
        "x_s": dma((4, n_x)),
        "x_r": dma((4, n_x)),
        "out_s": dma((tiles, n_x)),
        "out_r": dma((tiles, n_x)),
        "err_s": dma((4, n_x)),
        "err_r": dma((4, n_x)),
        "core_s": dma((2,)),
        "core_r": dma((2,)),
        "y_s": dma((2, n_y)),
        "y_r": dma((2, n_y)),
        "z_s": dma((n_z,)),
        "z_r": dma((n_z,)),
        "a0_s": dma((everyone,)),
        "a0_r": dma((everyone,)),
        "a1_s": dma((plane,)),
        "a1_r": dma((plane,)),
        "a2_s": dma((plane,)),
        "a2_r": dma((plane,)),
        "c2_s": dma((n_z,)),
        "c2_r": dma((n_z,)),
    }


class Refs:
    pass


def kernel(n_x, n_y, names, x_hbm, target_hbm, w_in_hbm, w_out_hbm, first_out, second_out, *scratch):
    s = Refs()
    for name, ref in zip(names, scratch):
        setattr(s, name, ref)
    n_z = 2 * n_y
    rows, width = x_hbm.shape
    hidden = w_in_hbm.shape[1]
    quarter = rows // n_x
    half, part, own = width // 2, width // (2 * n_y), width // (2 * n_y * n_z)
    width_tile, hidden_tile = tile_of(width), tile_of(hidden)

    me = lax.axis_index("dp")
    x = lax.axis_index("tensor")
    c = lax.rem(me, 2)
    y = lax.rem(lax.div(me, 2), n_y)
    z = lax.div(me, 2 * n_y)

    def dev(z_, y_, c_, x_):
        return {"dp": (z_ * n_y + y_) * 2 + c_, "tensor": x_}

    z_low = lax.rem(z, n_y)
    relay_dev = dev(z, lax.rem(y + z_low, n_y), 1 - c, x)
    relayed_y = lax.rem(y - z_low + n_y, n_y)
    relayed_dev = dev(z, relayed_y, 1 - c, x)
    final_dev = dev((1 - c) * n_y + relayed_y, y, lax.div(z, n_y), x)
    from_core = lax.div(z, n_y)
    from_y = lax.rem(z, n_y)
    y_node = lax.rem(y - from_y + n_y, n_y)
    source_dev = dev(c * n_y + y_node, y, 1 - from_core, x)
    z_node = from_y * 2 + from_core

    def x_peer(k):
        return dev(z, y, c, lax.rem(x + k, n_x))

    def group_peer(k):
        return dev(z, y, lax.rem(c + k // n_x, 2), lax.rem(x + k % n_x, n_x))

    def plane_peer(k):
        group = k % (2 * n_x)
        return dev(
            z,
            lax.rem(y + k // (2 * n_x), n_y),
            lax.rem(c + group // n_x, 2),
            lax.rem(x + group % n_x, n_x),
        )

    def y_peer(k):
        return dev(z, lax.rem(y + k, n_y), c, x)

    def z_peer(k):
        return dev(lax.rem(z + k, n_z), y, c, x)

    fetch_in = pltpu.make_async_copy(w_in_hbm, s.w_in, s.local.at[0])
    fetch_out = pltpu.make_async_copy(w_out_hbm, s.w_out, s.local.at[1])
    fetch_in.start()
    fetch_out.start()

    barrier = pltpu.get_barrier_semaphore()
    everyone = [relay_dev, relayed_dev, final_dev, source_dev]
    everyone += [plane_peer(k) for k in range(1, 2 * n_x * n_y)]
    everyone += [z_peer(k) for k in range(1, n_z)]
    for peer in everyone:
        pl.semaphore_signal(barrier, inc=1, device_id=peer, device_id_type=MESH)
    pl.semaphore_wait(barrier, len(everyone))

    sent = []

    def push(src, dst, send_sem, recv_sem, peer):
        copy = pltpu.make_async_remote_copy(
            src_ref=src,
            dst_ref=dst,
            send_sem=send_sem,
            recv_sem=recv_sem,
            device_id=peer,
            device_id_type=MESH,
        )
        copy.start()
        sent.append(copy)
        return copy

    pieces = pieces_of(quarter)
    share = block(x * quarter, quarter, 16)
    x_from, target_from = x_hbm.at[share], target_hbm.at[share]
    hops = []
    for p, (start, size) in enumerate(pieces):
        at = pl.ds(start, size)
        hops.append(
            push(x_from.at[at], s.relay.at[at], s.hop1_s.at[p], s.hop1_r.at[p], relay_dev)
        )
    order_rows = tile_of(width)

    @pl.loop(0, width // order_rows)
    def _(step):
        base = step * order_rows
        i = lax.broadcasted_iota(jnp.int32, (order_rows, 128), 0) + base
        core_part = (i >= half).astype(jnp.int32)
        i = i - core_part * half
        y_part = jnp.zeros_like(i)
        for k in range(1, n_y):
            y_part = y_part + (i >= k * part).astype(jnp.int32)
        i = i - y_part * part
        z_part = jnp.zeros_like(i)
        for k in range(1, n_z):
            z_part = z_part + (i >= k * own).astype(jnp.int32)
        i = i - z_part * own
        column = ((z_part * n_y + y_part) * 2 + core_part) * own + i
        lanes = lax.broadcasted_iota(jnp.int32, (order_rows, 128), 1)
        for j in range(0, width, 128):
            size = min(128, width - j)
            hot = jnp.where(column == lanes + j, 1.0, 0.0)
            s.order[block(base, order_rows, 16), j : j + size] = hot[:, :size].astype(BF16)

    moved = []
    for p, (start, size) in enumerate(pieces):
        hops[p].wait_recv()
        moved.append(
            push(
                s.relay.at[pl.ds(start, size)],
                s.x.at[pl.ds(start, size)],
                s.hop2_s.at[p],
                s.hop2_r.at[p],
                final_dev,
            )
        )
    last_piece = len(pieces)
    hops.append(
        push(
            target_from,
            s.target_relay,
            s.hop1_s.at[last_piece],
            s.hop1_r.at[last_piece],
            relay_dev,
        )
    )

    fetch_out.wait()

    def reorder_w(t):
        cols = pl.ds(t * width_tile, width_tile)
        s.w_back[:, cols] = lax.dot_general(
            s.w_out[...], s.order[cols, :], BY_ROWS, preferred_element_type=F32
        ).astype(BF16)

    near = sorted({1, n_x - 1})
    groups = groups_of(n_x)
    slot = {k: i for i, k in enumerate(k for group in groups for k in group)}
    relays = [(p, near[p * len(near) // len(pieces)]) for p in (0, 2, 1, 3)]

    def rows_of(k, p):
        start, size = pieces[p]
        return pl.ds(slot[k] * quarter + start, size)

    def give(ref, p, send_sem, recv_sem):
        at = rows_of(0, p)
        return {
            (k, p): push(
                ref.at[at], ref.at[rows_of(k, p)], send_sem.at[p, k], recv_sem.at[p, k], x_peer(k)
            )
            for k in near
        }

    def relay(ref, given, send_sem, recv_sem):
        if n_x == 4:
            for p, k in relays:
                given[(k, p)].wait_recv()
                at = rows_of(k, p)
                given[(2, p)] = push(
                    ref.at[at],
                    ref.at[rows_of(2, p)],
                    send_sem.at[p, 2],
                    recv_sem.at[p, 2],
                    x_peer(k),
                )

    def take(given, k):
        for p in range(len(pieces)):
            if n_x < 4 or (p, k) not in relays:
                given[(k, p)].wait_recv()

    given = {}
    for p in range(len(pieces)):
        moved[p].wait_recv()
        given.update(give(s.x, p, s.x_s, s.x_r))
        if p < width // width_tile:
            reorder_w(p)
    for t in range(len(pieces), width // width_tile):
        reorder_w(t)

    fetch_in.wait()

    partials = []
    for turn, group in enumerate(groups):
        at = pl.ds(slot[group[0]] * quarter, len(group) * quarter)
        if turn == 1:
            relay(s.x, given, s.x_s, s.x_r)
            hops[last_piece].wait_recv()
            moved.append(
                push(
                    s.target_relay,
                    s.target,
                    s.hop2_s.at[last_piece],
                    s.hop2_r.at[last_piece],
                    final_dev,
                )
            )
        for k in group:
            if k:
                take(given, k)

        @pl.loop(0, hidden // hidden_tile)
        def _(j):
            cols = block(j * hidden_tile, hidden_tile, hidden_tile)
            v = jnp.dot(s.x[at, :], s.w_in[:, cols], preferred_element_type=F32)
            v2 = v * v
            t = jnp.tanh(GELU_A * (v + GELU_B * (v * v2)))
            s.hid[at, cols] = (0.5 * v * (1.0 + t)).astype(BF16)
            s.slope[at, cols] = 0.5 * (1.0 + t) + (0.5 * v) * (1.0 - t * t) * (
                GELU_A * (1.0 + (3.0 * GELU_B) * v2)
            )

        for t in range(width // width_tile):
            cols = pl.ds(t * width_tile, width_tile)
            o = jnp.dot(s.hid[at, :], s.w_back[:, cols], preferred_element_type=F32)
            for i, k in enumerate(group):
                if k == 0:
                    s.out_own[:, cols] = o
                    continue
                s.out_send[k - 1, t] = o[i * quarter : (i + 1) * quarter].astype(BF16)
                partials.append(
                    push(
                        s.out_send.at[k - 1, t],
                        s.out_recv.at[k - 1, t],
                        s.out_s.at[t, k],
                        s.out_r.at[t, k],
                        x_peer(n_x - k),
                    )
                )

    @pl.loop(0, width // order_rows)
    def _(step):
        at = block(step * order_rows, order_rows, 16)
        s.x_t[at, :] = lax.dot_general(
            s.order[at, :], s.x[...], BY_ROWS, preferred_element_type=F32
        ).astype(BF16)

    moved[last_piece].wait_recv()

    @pl.loop(0, width // width_tile)
    def _(j):
        cols = block(j * width_tile, width_tile, width_tile)
        s.target_back[:, cols] = lax.dot_general(
            s.target[...], s.order[cols, :], BY_ROWS, preferred_element_type=F32
        ).astype(BF16)

    for copy in partials:
        copy.wait_recv()

    @pl.loop(0, quarter // 16)
    def _(i):
        at = block(i * 16, 16, 16)
        for t in range(width // width_tile):
            cols = pl.ds(t * width_tile, width_tile)
            total = s.out_own[at, cols]
            for k in range(1, n_x):
                total = total + s.out_recv[k - 1, t, at, :].astype(F32)
            error = (total - s.target_back[at, cols].astype(F32)) / rows
            s.err[at, cols] = error.astype(BF16)

    given = {}
    for p in range(len(pieces)):
        given.update(give(s.err, p, s.err_s, s.err_r))
    mine = block(c * half, half, 16)
    theirs = block((1 - c) * half, half, 16)
    partner = dev(z, y, 1 - c, x)
    crossed = []

    def cross(m):
        crossed.append(push(s.send.at[m], s.recv.at[m], s.core_s.at[m], s.core_r.at[m], partner))

    def gradient_first(at, store):
        @pl.loop(0, hidden // hidden_tile)
        def _(j):
            cols = block(j * hidden_tile, hidden_tile, hidden_tile)
            store(cols, jnp.dot(s.x_t[at, :], s.dpre[:, cols], preferred_element_type=F32))

    def store_send(cols, value):
        s.send[0, :, cols] = value.astype(BF16)

    def store_keep(cols, value):
        s.keep[:, cols] = value

    for turn, group in enumerate(groups):
        at = pl.ds(slot[group[0]] * quarter, len(group) * quarter)
        err_t = getattr(s, f"err_t{turn}")
        if turn == 1:
            relay(s.err, given, s.err_s, s.err_r)
        for k in group:
            if k:
                take(given, k)

        @pl.loop(0, hidden // hidden_tile)
        def _(j):
            cols = block(j * hidden_tile, hidden_tile, hidden_tile)
            back = lax.dot_general(
                s.err[at, :], s.w_back[cols, :], BY_ROWS, preferred_element_type=F32
            )
            s.dpre[at, cols] = (back * s.slope[at, cols]).astype(BF16)

        last = turn == len(groups) - 1
        if last:
            gradient_first(theirs, store_send)
            cross(0)

        for t in range(width // width_tile):
            cols = pl.ds(t * width_tile, width_tile)
            err_t[cols, :] = s.err[at, cols].T

        @pl.loop(0, hidden // hidden_tile)
        def _(j):
            cols = block(j * hidden_tile, hidden_tile, hidden_tile)
            if last:
                s.send[1, :, cols] = (
                    s.second[theirs, cols]
                    + jnp.dot(err_t[theirs, :], s.hid[at, cols], preferred_element_type=F32)
                ).astype(BF16)
                s.second[mine, cols] += jnp.dot(
                    err_t[mine, :], s.hid[at, cols], preferred_element_type=F32
                )
            else:
                value = jnp.dot(err_t[...], s.hid[at, cols], preferred_element_type=F32)
                if turn == 0:
                    s.second[:, cols] = value
                else:
                    s.second[:, cols] += value

        if last:
            cross(1)
            gradient_first(mine, store_keep)

    def own_part(m, start):
        if m == 0:
            return s.keep[block(start, 16, 16), :]
        return s.second[block(c * half + start, 16, 16), :]

    def total_over(buffer, send_sem, recv_sem, peer_of, count):
        copies = [
            push(buffer.at[0], buffer.at[k], send_sem.at[k], recv_sem.at[k], peer_of(k))
            for k in range(1, count)
        ]
        for copy in copies:
            copy.wait_recv()
        total = buffer[0]
        for k in range(1, count):
            total = total + buffer[k]
        return total

    stats = (jnp.zeros((8, 128), F32),) * 3
    for m in range(2):
        crossed[m].wait_recv()

        def level_sums(i, carry):
            at = block(i * 16, 16, 16)
            a = own_part(m, i * 16)
            b = s.recv[m, at, :].astype(F32)
            return (carry[0] + fold(a * b), carry[1] + fold(a * a), carry[2] + fold(b * b))

        stats = lax.fori_loop(0, half // 16, level_sums, stats)
    is_low = c == 0
    s.a0[0] = pack(
        s.r0,
        (
            stats[0],
            jnp.where(is_low, stats[1], stats[2]),
            jnp.where(is_low, stats[2], stats[1]),
        ),
    )
    total = total_over(s.a0, s.a0_s, s.a0_r, group_peer, 2 * n_x)
    weights = tree_weights(unpack(total, ((0, 1), (0, 0), (1, 1)), 8), 2)
    weight_own = jnp.where(is_low, weights[0], weights[1])
    weight_other = jnp.where(is_low, weights[1], weights[0])

    y_copies = [[], []]
    for m in range(2):
        for k in list(range(1, n_y)) + [0]:
            part_at = lax.rem(y + k, n_y) * part

            @pl.loop(0, part // 16)
            def _(i):
                at = block(part_at + i * 16, 16, 16)
                node = weight_own * own_part(m, part_at + i * 16)
                node = (node + weight_other * s.recv[m, at, :].astype(F32)).astype(BF16)
                if k:
                    s.node[m, at, :] = node
                else:
                    s.y_recv[y_node, m, block(i * 16, 16, 16), :] = node

            if k:
                y_copies[m].append(
                    push(
                        s.node.at[m, block(part_at, part, 16)],
                        s.y_recv.at[y_node, m],
                        s.y_s.at[m, k],
                        s.y_r.at[m, k],
                        y_peer(k),
                    )
                )

    y_pairs = pairs_of(n_y)

    stats = (jnp.zeros((8, 128), F32),) * len(y_pairs)
    for m in range(2):
        for copy in y_copies[m]:
            copy.wait_recv()

        def y_sums(i, carry):
            at = block(i * 16, 16, 16)
            nodes = [s.y_recv[j, m, at, :].astype(F32) for j in range(n_y)]
            return tuple(old + fold(nodes[a] * nodes[b]) for old, (a, b) in zip(carry, y_pairs))

        stats = lax.fori_loop(0, part // 16, y_sums, stats)
    s.a1[0] = pack(s.r1, stats)
    total = total_over(s.a1, s.a1_s, s.a1_r, plane_peer, 2 * n_x * n_y)
    weights = tree_weights(unpack(total, y_pairs, s.r1.shape[0]), n_y)

    @pl.loop(0, part // 16)
    def _(i):
        at = block(i * 16, 16, 16)
        for m in range(2):
            merged = weights[0] * s.y_recv[0, m, at, :].astype(F32)
            for j in range(1, n_y):
                merged = merged + weights[j] * s.y_recv[j, m, at, :].astype(F32)
            s.y_merged[m, at, :] = merged

    for j in range(n_z):
        for m in range(2):
            s.z_send[j, m] = s.y_merged[m, j * own : (j + 1) * own, :].astype(BF16)

    z_copies = []
    for k in range(1, n_z):
        z_copies.append(
            push(
                s.z_send.at[lax.rem(z + k, n_z)],
                s.z_recv.at[z_node],
                s.z_s.at[k],
                s.z_r.at[k],
                z_peer(k),
            )
        )
    s.z_recv[z_node] = s.z_send[z]
    for copy in z_copies:
        copy.wait_recv()

    z_pairs = pairs_of(n_z)
    stats = []
    for a, b in z_pairs:
        value = 0.0
        for m in range(2):
            value = value + s.z_recv[a, m].astype(F32) * s.z_recv[b, m].astype(F32)
        stats.append(fold_row(value))
    s.a2[0] = pack(s.r2, stats)
    s.c2[0] = total_over(s.a2, s.a2_s, s.a2_r, plane_peer, 2 * n_x * n_y)
    total = total_over(s.c2, s.c2_s, s.c2_r, z_peer, n_z)
    weights = tree_weights(unpack(total, z_pairs, s.r2.shape[0]), n_z)
    for m, out in enumerate((first_out, second_out)):
        merged = weights[0] * s.z_recv[0, m].astype(F32)
        for j in range(1, n_z):
            merged = merged + weights[j] * s.z_recv[j, m].astype(F32)
        out[...] = merged
    for copy in sent:
        copy.wait_send()


def solution(mesh):
    n_x = mesh.shape["tensor"]
    n_y = math.isqrt(mesh.shape["dp"] // 4)

    def on_device(inputs, targets, w_in, w_out):
        rows, width = inputs.shape
        hidden = w_in.shape[1]
        scratch = scratch_of(n_x, n_y, rows, width, hidden)
        share = jax.ShapeDtypeStruct((width // mesh.shape["dp"], hidden), F32)
        return pl.pallas_call(
            functools.partial(kernel, n_x, n_y, tuple(scratch)),
            out_shape=(share, share),
            in_specs=[pl.BlockSpec(memory_space=pl.ANY)] * 4,
            out_specs=(pl.BlockSpec(memory_space=pltpu.VMEM),) * 2,
            scratch_shapes=list(scratch.values()),
            compiler_params=pltpu.CompilerParams(
                collective_id=0, has_side_effects=True, vmem_limit_bytes=67_000_000
            ),
        )(inputs, targets, w_in, w_out)

    placed = (P("dp", None), P("dp", None), P(None, "tensor"), P("tensor", None))
    return jax.shard_map(
        on_device,
        mesh=mesh,
        in_specs=placed,
        out_specs=(P("dp", "tensor"), P("dp", "tensor")),
        check_vma=False,
    )
```
